128 devices in a mesh: tm: 32 (over y, x_hi, z), chan: 4 (over x_lo, core).
Axes of the slice: x: 4 (x_hi: 2, x_lo: 2; x = x_hi * 2 + x_lo), y: 4, z: 4, core: 2. Of those that a mesh axis runs over, the one named last changes fastest.
Arguments:
- series: float32 [256, 8192], P('chan', 'tm'), may hold values from -6 to 6
- lengths: int32 [64], replicated, may hold values from 42 to 128
Outputs:
- peak: float32 [8192], P('tm')
The draws below stay inside these ranges and needn't reach their ends.
All inputs are finite; a program needn't handle non-finite values.
Results may differ from the reference program's by a relative error of at most 0.0015.
Values may be sent and summed in bfloat16 or wider, within the bound.
No kernel may reach another device: no remote copies, remote signals or barrier semaphores. Data moves between devices by JAX's collectives and lax.ppermute only.
A program may use at most 128 MiB of HBM per device.

```python
import jax
import jax.numpy as jnp
from jax import lax

C = 256
WIN = 256
ROWS_DEV = 256
STEPS = 2
ROWS = 8192
NSEG = 64
N_TM = 32


def with_ends(drawn, own_key, low, largest):
    longest = drawn.shape.index(max(drawn.shape))
    spots = []
    for shift in (0, 1):
        where = [jax.random.randint(jax.random.fold_in(own_key, axis), (), 0, length) for axis, length in enumerate(drawn.shape)]
        where[longest] = (where[longest] + shift) % drawn.shape[longest]
        spots.append(tuple(where))
    return drawn.at[spots[0]].set(low).at[spots[1]].set(largest)


def block_scale(key, shape, shards, smallest, top_value):
    factor_of = 1.0
    for axis_at, shards_of in shards:
        draws = jax.random.uniform(jax.random.fold_in(jax.random.fold_in(key, 6), axis_at), (shards_of,), jnp.float32, smallest / len(shards), top_value / len(shards))
        factor_of = factor_of * jnp.repeat(jnp.exp(draws), shape[axis_at] // shards_of).reshape((-1,) + (1,) * (len(shape) - 1 - axis_at))
    return factor_of


def normal_values(key, extent, width, bound, pieces=(), held_as=jnp.bfloat16):
    array = jax.random.normal(key, extent, jnp.float32) * width
    if len(pieces) > 0:
        array = block_scale(key, extent, pieces, -0.22, 0.18) * array
    return jnp.clip(array, min=-bound, max=bound).astype(held_as)


def setup_inputs(seed: int = 0) -> dict:
    key_list = jax.random.split(jax.random.key(seed), 3)
    series = normal_values(key_list[0], (C, ROWS), 1.0, 6.0, ((0, 4), (1, 32)), jnp.float32)
    lengths = with_ends(jax.random.randint(key_list[1], (NSEG,), ROWS_DEV // 6, ROWS_DEV // 2 + 1), jax.random.fold_in(key_list[1], 1), ROWS_DEV // 6, (ROWS_DEV // 2 + 1) - 1).astype(jnp.int32)
    return {"series": series, "lengths": lengths}


EPS = 1e-05
MASKED = -1000000000.0

def windows_of(extended):
    count = extended.shape[1] - WIN + 1
    starts = jnp.arange(count, dtype=jnp.int32)
    index = starts[:, None] + jnp.arange(WIN, dtype=jnp.int32)[None, :]
    stacked = jnp.transpose(extended[:, index], (1, 0, 2))
    center = stacked - lax.optimization_barrier(jnp.mean(stacked, axis=2, keepdims=True))
    spread = lax.optimization_barrier(jnp.mean(center * center, axis=2, keepdims=True))
    normed = center * lax.rsqrt(spread + EPS)
    return normed.reshape(count, -1).astype(jnp.bfloat16)

def validity(block, lengths, rows, total):
    local = jnp.arange(rows, dtype=jnp.int32)
    seg_len = rows // 2
    pair = lax.dynamic_slice_in_dim(lengths, (block * 2).astype(jnp.int32), 2)
    limit = jnp.where(local < seg_len, pair[0], pair[1])
    offset = local % seg_len
    return (offset < limit) & (block * rows + local <= total - WIN)

def reference(series, lengths):
    total = series.shape[1]
    padded = jnp.concatenate([series, jnp.zeros((series.shape[0], WIN - 1), series.dtype)], axis=1)
    excl = WIN // 4

    def block_windows(block):
        start = (block * ROWS_DEV).astype(jnp.int32)
        return windows_of(lax.dynamic_slice_in_dim(padded, start, ROWS_DEV + WIN - 1, 1))

    def row_block(block):
        rows_z = block_windows(block)
        rows_ok = validity(block, lengths, ROWS_DEV, total)
        local = jnp.arange(ROWS_DEV, dtype=jnp.int32)
        best = jnp.full((ROWS_DEV,), MASKED, jnp.float32)
        for step in range(STEPS + 1):
            other = block - step
            safe = jnp.maximum(other, 0)
            cols_z = block_windows(safe)
            cols_ok = validity(safe, lengths, ROWS_DEV, total) & (other >= 0)
            score = lax.dot_general(rows_z, cols_z, (((1,), (1,)), ((), ())), preferred_element_type=jnp.float32) * (1.0 / WIN)
            lag = step * ROWS_DEV + local[:, None] - local[None, :]
            keep = rows_ok[:, None] & cols_ok[None, :] & (lag >= excl)
            best = jnp.maximum(best, lax.optimization_barrier(jnp.max(jnp.where(keep, score, MASKED), axis=1)))
        return jnp.where(best > 0.5 * MASKED, best, 0.0).astype(jnp.float32)
    blocks = lax.map(row_block, jnp.arange(N_TM, dtype=jnp.int32))
    return blocks.reshape(total)
```

```python
import functools

import jax
import jax.numpy as jnp
from jax import lax
from jax.experimental import pallas as pl
from jax.experimental.pallas import tpu as pltpu
from jax.sharding import PartitionSpec as P

WIN = 256
HALF = WIN // 2
STEPS = 2
EPS = 1e-05
MASKED = -1000000000.0
EXCL = WIN // 4
KC = 16


def shifted(block, axis, distance):
    devices = range(lax.axis_size(axis))
    route = [(i - distance, i) for i in devices if i - distance in devices]
    return lax.ppermute(block, axis, route)


def swapped(block, axis, distance):
    count = lax.axis_size(axis)
    return lax.ppermute(block, axis, [(i, (i + distance) % count) for i in range(count)])


def corr_kernel(rows, cols, b2, b1, b0, bn, out, x2, ma, mb, va, vb, za, zb, acc):
    total = (STEPS + 1) * rows
    span = total + HALF
    joined = jnp.concatenate([b2[...], b1[...], b0[...], bn[...]], axis=1)
    both = jnp.concatenate([joined[:, :span], joined[:, HALF : HALF + span]], axis=0)
    for at in range(0, span, 128):
        x2[at : at + 128, :] = both[:, at : at + 128].T

    size = 128
    pieces = span // size
    length = 1
    src_m, src_v = x2, None
    bufs = [(ma, va), (mb, vb)]
    level = 0
    while length < HALF:
        dst_m, dst_v = bufs[level % 2]

        def step(p, carry, src_m=src_m, src_v=src_v, dst_m=dst_m, dst_v=dst_v, length=length):
            base = pl.multiple_of(p * size, size)
            m0 = src_m[pl.ds(base, size), :]
            m1 = src_m[pl.ds(base + length, size), :]
            gap = m0 - m1
            spread = gap * gap * (0.5 * length)
            if src_v is not None:
                spread = spread + (src_v[pl.ds(base, size), :] + src_v[pl.ds(base + length, size), :])
            dst_m[pl.ds(base, size), :] = (m0 + m1) * 0.5
            dst_v[pl.ds(base, size), :] = spread
            return carry

        lax.fori_loop(0, pieces, step, 0)
        src_m, src_v = dst_m, dst_v
        length *= 2
        level += 1
    end_m, end_v = bufs[level % 2]
    for at in range(0, total, size):
        m0 = src_m[at : at + size, :]
        v0 = src_v[at : at + size, :]
        m1 = pltpu.roll(m0, 64, 1)
        v1 = pltpu.roll(v0, 64, 1)
        gap = m0 - m1
        var = (v0 + v1 + gap * gap * (0.5 * HALF)) * (1.0 / WIN)
        end_m[at : at + size, :] = (m0 + m1) * 0.5
        end_v[at : at + size, :] = lax.rsqrt(var + EPS)

    group = 64

    def build(chunk, z):
        base = pl.multiple_of(chunk * KC, KC)
        for at in range(0, total, group):
            mean = end_m[at : at + group, :]
            scale = end_v[at : at + group, :]
            for k in range(KC):
                x = x2[pl.ds(base + (at + k), group), :]
                z[at : at + group, k * 128 : (k + 1) * 128] = ((x - mean) * scale).astype(jnp.bfloat16)

    def product(z):
        acc[...] += lax.dot_general(
            z[:cols, :], z[total - rows :, :], (((1,), (1,)), ((), ())), preferred_element_type=jnp.float32
        )

    acc[...] = jnp.zeros_like(acc)
    chunks = HALF // KC
    build(0, za)

    def pair(p, carry):
        build(2 * p + 1, zb)
        product(za)
        build(2 * p + 2, za)
        product(zb)
        return carry

    lax.fori_loop(0, chunks // 2 - 1, pair, 0)
    build(chunks - 1, zb)
    product(za)
    product(zb)
    out[...] = acc[...].astype(out.dtype)


def peak_kernel(rows, quarter, lens, p0, p1, p2, p3, out):
    block = lax.axis_index("tm")
    part = lax.axis_index("chan")
    total_rows = rows * lax.axis_size("tm")
    seg = rows // 2
    n_seg = 2 * (STEPS + 1)
    summed = (p0[...].astype(jnp.float32) + p1[...].astype(jnp.float32)) + (
        p2[...].astype(jnp.float32) + p3[...].astype(jnp.float32)
    )
    score = summed * (1.0 / WIN)
    shape = score.shape
    j = part * quarter + lax.broadcasted_iota(jnp.int32, shape, 0)
    i = STEPS * rows + lax.broadcasted_iota(jnp.int32, shape, 1)
    first = (block - STEPS) * rows
    limit = jnp.zeros(shape, jnp.int32)
    for s in range(n_seg):
        which = (block - STEPS) * 2 + s
        here = lens[jnp.maximum(which, 0)]
        here = jnp.where(which >= 0, here, 0)
        limit = jnp.where(j // seg == s, here, limit)
    last = total_rows - WIN
    ok = (j % seg < limit) & (j + first <= last) & (i - j >= EXCL)
    best = jnp.max(jnp.where(ok, score, MASKED), axis=0, keepdims=True)
    r = lax.broadcasted_iota(jnp.int32, best.shape, 1)
    own = jnp.where(r < seg, lens[block * 2], lens[block * 2 + 1])
    row_ok = (r % seg < own) & (block * rows + r <= last)
    out[...] = jnp.where(row_ok, best, MASKED)


def body(series, lengths):
    chans, rows = series.shape
    parts = lax.axis_size("chan")
    total = (STEPS + 1) * rows
    cols = total - EXCL
    quarter = cols // parts
    b1 = shifted(series, "tm", 1)
    b2 = shifted(series, "tm", 2)
    bn = shifted(series, "tm", -1)
    vmem = pl.BlockSpec(memory_space=pltpu.VMEM)
    f32 = jnp.float32
    room = total + HALF + HALF
    partial_value = pl.pallas_call(
        functools.partial(corr_kernel, rows, cols),
        out_shape=jax.ShapeDtypeStruct((cols, rows), f32),
        in_specs=[vmem] * 4,
        out_specs=vmem,
        scratch_shapes=[pltpu.VMEM((room, 128), f32)] * 5
        + [pltpu.VMEM((total, KC * 128), jnp.bfloat16)] * 2
        + [pltpu.VMEM((cols, rows), f32)],
        compiler_params=pltpu.CompilerParams(vmem_limit_bytes=40 << 20),
    )(b2, b1, series, bn)
    pieces = partial_value.reshape(parts, quarter, rows)
    got = lax.all_to_all(pieces, "chan", 0, 0, tiled=True)
    best = pl.pallas_call(
        functools.partial(peak_kernel, rows, quarter),
        out_shape=jax.ShapeDtypeStruct((1, rows), f32),
        in_specs=[pl.BlockSpec(memory_space=pltpu.SMEM)] + [vmem] * 4,
        out_specs=vmem,
    )(lengths, got[0], got[1], got[2], got[3])
    best = best.reshape(rows)
    others = [swapped(best, "chan", d) for d in range(1, parts)]
    for other in others:
        best = jnp.maximum(best, other)
    return jnp.where(best > 0.5 * MASKED, best, 0.0)


def solution(mesh):
    return jax.shard_map(
        body,
        mesh=mesh,
        in_specs=(P("chan", "tm"), P()),
        out_specs=P("tm"),
        check_vma=False,
    )
```

```python
import functools

import jax
import jax.numpy as jnp
from jax import lax
from jax.experimental import pallas as pl
from jax.experimental.pallas import tpu as pltpu
from jax.sharding import PartitionSpec as P

WIN = 256
HALF = WIN // 2
STEPS = 2
EPS = 1e-05
MASKED = -1000000000.0
EXCL = WIN // 4
KC = 16
LANES = 128
VMEM_LIMIT = 40 << 20
SMALL_LIMIT = 8 << 20


def sent(block, axis, target):
    count = lax.axis_size(axis)
    return lax.ppermute(block, axis, [(i, target(i, count)) for i in range(count)])


def two_on(i, count):
    return (i + 2) % count


def even_pair(i, count):
    return i ^ 1


def odd_pair(i, count):
    if i == 0 or i == count - 1:
        return i
    return i + 1 if i % 2 == 1 else i - 1


def turned(distance):
    return lambda i, count: (i + distance) % count


def window_sums(src_m, bufs, span):
    size = 128
    src_v = None
    length = 1
    level = 0
    while length < HALF:
        dst_m, dst_v = bufs[level % 2]

        def step(p, carry, src_m=src_m, src_v=src_v, dst_m=dst_m, dst_v=dst_v, length=length):
            base = pl.multiple_of(p * size, size)
            m0 = src_m[pl.ds(base, size), :]
            m1 = src_m[pl.ds(base + length, size), :]
            gap = m0 - m1
            spread = gap * gap * (0.5 * length)
            if src_v is not None:
                spread = spread + (src_v[pl.ds(base, size), :] + src_v[pl.ds(base + length, size), :])
            dst_m[pl.ds(base, size), :] = (m0 + m1) * 0.5
            dst_v[pl.ds(base, size), :] = spread
            return carry

        lax.fori_loop(0, span // size, step, 0)
        src_m, src_v = dst_m, dst_v
        length *= 2
        level += 1
    return src_m, src_v, bufs[level % 2]


def corr_kernel(rows, cols, own_far, odd_side, b2, even_side, *refs):
    outs, (own, arrived, x2, ma, mb, va, vb, za, zb, acc) = refs[:4], refs[4:]
    fetch = pltpu.make_async_copy(own_far, own, arrived)
    fetch.start()
    total = (STEPS + 1) * rows
    span = total + HALF
    odd = lax.rem(lax.axis_index("tm"), 2) == 1
    from_odd, from_even = odd_side[...], even_side[...]
    before = jnp.where(odd, from_even, from_odd)
    after = jnp.where(odd, from_odd, from_even)
    fetch.wait()
    joined = jnp.concatenate([b2[...], before, own[...], after], axis=1)
    both = jnp.concatenate([joined[:, :span], joined[:, HALF : HALF + span]], axis=0)
    for at in range(0, span, LANES):
        x2[at : at + LANES, :] = both[:, at : at + LANES].T

    src_m, src_v, (end_m, end_v) = window_sums(x2, [(ma, va), (mb, vb)], span)
    for at in range(0, total, LANES):
        m0 = src_m[at : at + LANES, :]
        v0 = src_v[at : at + LANES, :]
        m1 = pltpu.roll(m0, LANES // 2, 1)
        v1 = pltpu.roll(v0, LANES // 2, 1)
        gap = m0 - m1
        var = (v0 + v1 + gap * gap * (0.5 * HALF)) * (1.0 / WIN)
        end_m[at : at + LANES, :] = (m0 + m1) * 0.5
        end_v[at : at + LANES, :] = lax.rsqrt(var + EPS)

    group = 64

    def build(chunk, z):
        base = pl.multiple_of(chunk * KC, KC)
        for at in range(0, total, group):
            mean = end_m[at : at + group, :]
            scale = end_v[at : at + group, :]
            for k in range(KC):
                x = x2[pl.ds(base + (at + k), group), :]
                z[at : at + group, k * LANES : (k + 1) * LANES] = ((x - mean) * scale).astype(jnp.bfloat16)

    def product(z):
        acc[...] += lax.dot_general(
            z[:cols, :], z[total - rows :, :], (((1,), (1,)), ((), ())), preferred_element_type=jnp.float32
        )

    acc[...] = jnp.zeros_like(acc)
    chunks = HALF // KC
    build(0, za)

    def pair(p, carry):
        build(2 * p + 1, zb)
        product(za)
        build(2 * p + 2, za)
        product(zb)
        return carry

    lax.fori_loop(0, chunks // 2 - 1, pair, 0)
    build(chunks - 1, zb)
    product(za)
    product(zb)
    part = lax.axis_index("chan")
    for d, out in enumerate(outs):
        which = lax.rem(part + d, len(outs))
        size = out.shape[0]
        out[...] = acc[pl.ds(pl.multiple_of(which * size, 16), size), :].astype(out.dtype)


def peak_kernel(rows, lens, p0, p1, p2, p3, out):
    quarter = p0.shape[0]
    block = lax.axis_index("tm")
    part = lax.axis_index("chan")
    last = rows * lax.axis_size("tm") - WIN
    seg = rows // 2
    start = (block - STEPS) * rows
    f32 = jnp.float32
    score = (p0[...] + p1[...].astype(f32)) + (p2[...].astype(f32) + p3[...].astype(f32))
    shape = (quarter, LANES)
    j = part * quarter + lax.broadcasted_iota(jnp.int32, shape, 0)
    stop = jnp.zeros(shape, jnp.int32)
    for s in range(2 * (STEPS + 1)):
        which = (block - STEPS) * 2 + s
        length = jnp.where(which >= 0, lens[jnp.maximum(which, 0)], 0)
        end = jnp.minimum(s * seg + length, last + 1 - start)
        stop = jnp.where(j >= s * seg, end, stop)
    reach = jnp.where(j < stop, j + EXCL, 2 * (STEPS + 1) * rows)
    lane = lax.broadcasted_iota(jnp.int32, shape, 1)
    for at in range(0, rows, LANES):
        i = lane + (STEPS * rows + at)
        best = jnp.max(jnp.where(i >= reach, score[:, at : at + LANES], MASKED), axis=0, keepdims=True)
        out[:, at : at + LANES] = best * (1.0 / WIN)


def close_kernel(rows, lens, a, b, c, d, out):
    block = lax.axis_index("tm")
    last = rows * lax.axis_size("tm") - WIN
    seg = rows // 2
    best = jnp.maximum(jnp.maximum(a[...], b[...]), jnp.maximum(c[...], d[...]))
    r = lax.broadcasted_iota(jnp.int32, best.shape, 1)
    stop = jnp.where(r < seg, lens[block * 2], seg + lens[block * 2 + 1])
    stop = jnp.minimum(stop, last + 1 - block * rows)
    floor = 0.5 * MASKED * (1.0 / WIN)
    out[...] = jnp.where((r < stop) & (best > floor), best, 0.0)


def body(series, lengths):
    chans, rows = series.shape
    parts = lax.axis_size("chan")
    total = (STEPS + 1) * rows
    cols = total - EXCL
    quarter = cols // parts
    b2 = sent(series, "tm", two_on)
    even_side = sent(series, "tm", even_pair)
    odd_side = sent(series, "tm", odd_pair)
    vmem = pl.BlockSpec(memory_space=pltpu.VMEM)
    smem = pl.BlockSpec(memory_space=pltpu.SMEM)
    f32 = jnp.float32
    bf16 = jnp.bfloat16
    room = total + HALF + HALF
    pieces = pl.pallas_call(
        functools.partial(corr_kernel, rows, cols),
        out_shape=[jax.ShapeDtypeStruct((quarter, rows), f32 if d == 0 else bf16) for d in range(parts)],
        in_specs=[pl.BlockSpec(memory_space=pltpu.HBM)] + [vmem] * 3,
        out_specs=[vmem] * parts,
        scratch_shapes=[pltpu.VMEM((chans, rows), f32), pltpu.SemaphoreType.DMA]
        + [pltpu.VMEM((room, LANES), f32)] * 5
        + [pltpu.VMEM((total, KC * LANES), bf16)] * 2
        + [pltpu.VMEM((cols, rows), f32)],
        compiler_params=pltpu.CompilerParams(vmem_limit_bytes=VMEM_LIMIT),
    )(series, odd_side, b2, even_side)
    got = [pieces[0]] + [sent(pieces[d], "chan", turned(d)) for d in range(1, parts)]
    best = pl.pallas_call(
        functools.partial(peak_kernel, rows),
        out_shape=jax.ShapeDtypeStruct((1, rows), f32),
        in_specs=[smem] + [vmem] * parts,
        out_specs=vmem,
        compiler_params=pltpu.CompilerParams(vmem_limit_bytes=SMALL_LIMIT),
    )(lengths, *got)
    all_best = [best] + [sent(best, "chan", turned(d)) for d in range(1, parts)]
    peak = pl.pallas_call(
        functools.partial(close_kernel, rows),
        out_shape=jax.ShapeDtypeStruct((1, rows), f32),
        in_specs=[smem] + [vmem] * parts,
        out_specs=vmem,
        compiler_params=pltpu.CompilerParams(vmem_limit_bytes=SMALL_LIMIT),
    )(lengths, *all_best)
    return peak.reshape(rows)


def solution(mesh):
    return jax.shard_map(
        body,
        mesh=mesh,
        in_specs=(P("chan", "tm"), P()),
        out_specs=P("tm"),
        check_vma=False,
    )
```

```python
import functools

import jax
import jax.numpy as jnp
from jax import lax
from jax.experimental import pallas as pl
from jax.experimental.pallas import tpu as pltpu
from jax.sharding import PartitionSpec as P

WIN = 256
HALF = WIN // 2
STEPS = 2
EPS = 1e-05
MASKED = -1000000000.0
EXCL = WIN // 4
KC = 16
LANES = 128
ALIGN = 8
VMEM_LIMIT = 40 << 20
SMALL_LIMIT = 8 << 20


def sent(block, axis, target):
    count = lax.axis_size(axis)
    return lax.ppermute(block, axis, [(i, target(i, count)) for i in range(count)])


def two_on(i, count):
    return (i + 2) % count


def even_pair(i, count):
    return i ^ 1


def odd_pair(i, count):
    if i == 0 or i == count - 1:
        return i
    return i + 1 if i % 2 == 1 else i - 1


def across(distance):
    return lambda i, count: i ^ distance


def window_sums(src_m, bufs, span):
    size = 128
    src_v = None
    length = 1
    level = 0
    while length < HALF:
        dst_m, dst_v = bufs[level % 2]

        def step(p, carry, src_m=src_m, src_v=src_v, dst_m=dst_m, dst_v=dst_v, length=length):
            base = pl.multiple_of(p * size, size)
            m0 = src_m[pl.ds(base, size), :]
            m1 = src_m[pl.ds(base + length, size), :]
            gap = m0 - m1
            spread = gap * gap * (0.5 * length)
            if src_v is not None:
                spread = spread + (src_v[pl.ds(base, size), :] + src_v[pl.ds(base + length, size), :])
            dst_m[pl.ds(base, size), :] = (m0 + m1) * 0.5
            dst_v[pl.ds(base, size), :] = spread
            return carry

        lax.fori_loop(0, span // size, step, 0)
        src_m, src_v = dst_m, dst_v
        length *= 2
        level += 1
    return src_m, src_v, bufs[level % 2]


def corr_kernel(rows, cols, own_far, odd_side, b2, even_side, *refs):
    outs, (own, arrived, x2, x8, ma, mb, va, vb, za, zb, acc) = refs[:4], refs[4:]
    fetch = pltpu.make_async_copy(own_far, own, arrived)
    fetch.start()
    total = (STEPS + 1) * rows
    span = total + HALF
    odd = lax.rem(lax.axis_index("tm"), 2) == 1
    from_odd, from_even = odd_side[...], even_side[...]
    before = jnp.where(odd, from_even, from_odd)
    after = jnp.where(odd, from_odd, from_even)
    fetch.wait()
    joined = jnp.concatenate([b2[...], before, own[...], after], axis=1)
    both = jnp.concatenate([joined[:, :span], joined[:, HALF : HALF + span]], axis=0)
    for at in range(0, span, LANES):
        x2[at : at + LANES, :] = both[:, at : at + LANES].T

    src_m, src_v, (end_m, end_v) = window_sums(x2, [(ma, va), (mb, vb)], span)
    for at in range(0, total, LANES):
        m0 = src_m[at : at + LANES, :]
        v0 = src_v[at : at + LANES, :]
        m1 = pltpu.roll(m0, LANES // 2, 1)
        v1 = pltpu.roll(v0, LANES // 2, 1)
        gap = m0 - m1
        var = (v0 + v1 + gap * gap * (0.5 * HALF)) * (1.0 / WIN)
        end_m[at : at + LANES, :] = (m0 + m1) * 0.5
        end_v[at : at + LANES, :] = lax.rsqrt(var + EPS)

    for s in range(ALIGN):
        for at in range(0, span, LANES):
            x8[s, at : at + LANES, :] = x2[at + s : at + s + LANES, :]

    group = 64

    def build(chunk, z):
        base = pl.multiple_of(chunk * KC, KC)
        for at in range(0, total, group):
            mean = end_m[at : at + group, :]
            scale = end_v[at : at + group, :]
            for k in range(KC):
                start = pl.multiple_of(base + (at + k // ALIGN * ALIGN), ALIGN)
                x = x8[k % ALIGN, pl.ds(start, group), :]
                z[at : at + group, k * LANES : (k + 1) * LANES] = ((x - mean) * scale).astype(jnp.bfloat16)

    def product(z):
        acc[...] += lax.dot_general(
            z[:cols, :], z[total - rows :, :], (((1,), (1,)), ((), ())), preferred_element_type=jnp.float32
        )

    acc[...] = jnp.zeros_like(acc)
    chunks = HALF // KC
    build(0, za)

    def pair(p, carry):
        build(2 * p + 1, zb)
        product(za)
        build(2 * p + 2, za)
        product(zb)
        return carry

    lax.fori_loop(0, chunks // 2 - 1, pair, 0)
    build(chunks - 1, zb)
    product(za)
    product(zb)
    part = lax.axis_index("chan")
    for d, out in enumerate(outs):
        which = part ^ d
        size = out.shape[0]
        out[...] = acc[pl.ds(pl.multiple_of(which * size, 16), size), :].astype(out.dtype)


def peak_kernel(rows, lens, p0, p1, p2, p3, out):
    quarter = p0.shape[0]
    block = lax.axis_index("tm")
    part = lax.axis_index("chan")
    last = rows * lax.axis_size("tm") - WIN
    seg = rows // 2
    start = (block - STEPS) * rows
    f32 = jnp.float32
    score = (p0[...] + p1[...]) + (p2[...].astype(f32) + p3[...].astype(f32))
    shape = (quarter, LANES)
    j = part * quarter + lax.broadcasted_iota(jnp.int32, shape, 0)
    stop = jnp.zeros(shape, jnp.int32)
    for s in range(2 * (STEPS + 1)):
        which = (block - STEPS) * 2 + s
        length = jnp.where(which >= 0, lens[jnp.maximum(which, 0)], 0)
        end = jnp.minimum(s * seg + length, last + 1 - start)
        stop = jnp.where(j >= s * seg, end, stop)
    reach = jnp.where(j < stop, j + EXCL, 2 * (STEPS + 1) * rows)
    lane = lax.broadcasted_iota(jnp.int32, shape, 1)
    for at in range(0, rows, LANES):
        i = lane + (STEPS * rows + at)
        best = jnp.max(jnp.where(i >= reach, score[:, at : at + LANES], MASKED), axis=0, keepdims=True)
        best = jnp.where(best > 0.5 * MASKED, best * (1.0 / WIN), MASKED)
        r = i[:1, :] - STEPS * rows
        own = jnp.where(r < seg, lens[block * 2], seg + lens[block * 2 + 1])
        out[:, at : at + LANES] = jnp.where(r < jnp.minimum(own, last + 1 - block * rows), best, MASKED)


def body(series, lengths):
    chans, rows = series.shape
    parts = lax.axis_size("chan")
    total = (STEPS + 1) * rows
    cols = total - EXCL
    quarter = cols // parts
    b2 = sent(series, "tm", two_on)
    even_side = sent(series, "tm", even_pair)
    odd_side = sent(series, "tm", odd_pair)
    vmem = pl.BlockSpec(memory_space=pltpu.VMEM)
    smem = pl.BlockSpec(memory_space=pltpu.SMEM)
    f32 = jnp.float32
    bf16 = jnp.bfloat16
    room = total + HALF + HALF
    pieces = pl.pallas_call(
        functools.partial(corr_kernel, rows, cols),
        out_shape=[jax.ShapeDtypeStruct((quarter, rows), f32 if d < 2 else bf16) for d in range(parts)],
        in_specs=[pl.BlockSpec(memory_space=pltpu.HBM)] + [vmem] * 3,
        out_specs=[vmem] * parts,
        scratch_shapes=[pltpu.VMEM((chans, rows), f32), pltpu.SemaphoreType.DMA, pltpu.VMEM((room, LANES), f32)]
        + [pltpu.VMEM((ALIGN, room, LANES), f32)]
        + [pltpu.VMEM((room, LANES), f32)] * 4
        + [pltpu.VMEM((total, KC * LANES), bf16)] * 2
        + [pltpu.VMEM((cols, rows), f32)],
        compiler_params=pltpu.CompilerParams(vmem_limit_bytes=VMEM_LIMIT),
    )(series, odd_side, b2, even_side)
    got = [pieces[0]] + [sent(pieces[d], "chan", across(d)) for d in range(1, parts)]
    best = pl.pallas_call(
        functools.partial(peak_kernel, rows),
        out_shape=jax.ShapeDtypeStruct((1, rows), f32),
        in_specs=[smem] + [vmem] * parts,
        out_specs=vmem,
        compiler_params=pltpu.CompilerParams(vmem_limit_bytes=SMALL_LIMIT),
    )(lengths, *got)
    peers = [sent(best, "chan", across(d)) for d in range(1, parts)]
    for peer in peers:
        best = jnp.maximum(best, peer)
    return jnp.where(best > 0.5 * MASKED, best, 0.0).reshape(rows)


def solution(mesh):
    return jax.shard_map(
        body,
        mesh=mesh,
        in_specs=(P("chan", "tm"), P()),
        out_specs=P("tm"),
        check_vma=False,
    )
```

```python
import functools

import jax
import jax.numpy as jnp
from jax import lax
from jax.experimental import pallas as pl
from jax.experimental.pallas import tpu as pltpu
from jax.sharding import PartitionSpec as P

WIN = 256
HALF = WIN // 2
STEPS = 2
EPS = 1e-05
MASKED = -1000000000.0
EXCL = WIN // 4
STEP_K = 4
GROUP = 64
LANES = 128
ALIGN = 8
VMEM_LIMIT = 40 << 20
SMALL_LIMIT = 8 << 20


def sent(block, axis, target):
    count = lax.axis_size(axis)
    return lax.ppermute(block, axis, [(i, target(i, count)) for i in range(count)])


def two_on(i, count):
    return (i + 2) % count


def even_pair(i, count):
    return i ^ 1


def odd_pair(i, count):
    if i == 0 or i == count - 1:
        return i
    return i + 1 if i % 2 == 1 else i - 1


def across(distance):
    return lambda i, count: i ^ distance


def window_sums(src_m, bufs, span):
    size = 128
    src_v = None
    length = 1
    level = 0
    while length < HALF:
        dst_m, dst_v = bufs[level % 2]

        def step(p, carry, src_m=src_m, src_v=src_v, dst_m=dst_m, dst_v=dst_v, length=length):
            base = pl.multiple_of(p * size, size)
            m0 = src_m[pl.ds(base, size), :]
            m1 = src_m[pl.ds(base + length, size), :]
            gap = m0 - m1
            spread = gap * gap * (0.5 * length)
            if src_v is not None:
                spread = spread + (src_v[pl.ds(base, size), :] + src_v[pl.ds(base + length, size), :])
            dst_m[pl.ds(base, size), :] = (m0 + m1) * 0.5
            dst_v[pl.ds(base, size), :] = spread
            return carry

        lax.fori_loop(0, span // size, step, 0)
        src_m, src_v = dst_m, dst_v
        length *= 2
        level += 1
    return src_m, src_v, bufs[level % 2]


def corr_kernel(rows, cols, own_far, odd_side, b2, even_side, *refs):
    outs, (own, arrived, x2, x8, ma, mb, va, vb, zr, acc) = refs[:4], refs[4:]
    fetch = pltpu.make_async_copy(own_far, own, arrived)
    fetch.start()
    total = (STEPS + 1) * rows
    span = total + HALF
    odd = lax.rem(lax.axis_index("tm"), 2) == 1
    from_odd, from_even = odd_side[...], even_side[...]
    before = jnp.where(odd, from_even, from_odd)
    after = jnp.where(odd, from_odd, from_even)
    fetch.wait()
    joined = jnp.concatenate([b2[...], before, own[...], after], axis=1)
    both = jnp.concatenate([joined[:, :span], joined[:, HALF : HALF + span]], axis=0)
    for at in range(0, span, LANES):
        x2[at : at + LANES, :] = both[:, at : at + LANES].T

    src_m, src_v, (end_m, end_v) = window_sums(x2, [(ma, va), (mb, vb)], span)
    for at in range(0, total, LANES):
        m0 = src_m[at : at + LANES, :]
        v0 = src_v[at : at + LANES, :]
        m1 = pltpu.roll(m0, LANES // 2, 1)
        v1 = pltpu.roll(v0, LANES // 2, 1)
        gap = m0 - m1
        var = (v0 + v1 + gap * gap * (0.5 * HALF)) * (1.0 / WIN)
        end_m[at : at + LANES, :] = (m0 + m1) * 0.5
        end_v[at : at + LANES, :] = lax.rsqrt(var + EPS)

    for s in range(ALIGN):
        for at in range(0, span, LANES):
            x8[s, at : at + LANES, :] = x2[at + s : at + s + LANES, :]

    def windows(at, size, step):
        mean = end_m[at : at + size, :]
        scale = end_v[at : at + size, :]
        lag = lax.rem(step, 2) * STEP_K
        start = pl.multiple_of(step // 2 * ALIGN + at, ALIGN)
        z = []
        for k in range(STEP_K):
            x = x8[lag + k, pl.ds(start, size), :]
            z.append(((x - mean) * scale).astype(jnp.bfloat16))
        return jnp.concatenate(z[:2], axis=1), jnp.concatenate(z[2:], axis=1)

    first_row = total - rows

    def stage(step):
        slot = lax.rem(step, 2)
        for at in range(0, rows, GROUP):
            for unit, z in enumerate(windows(first_row + at, GROUP, step)):
                zr[slot, unit, at : at + GROUP, :] = z
        for unit in range(2):
            pltpu.matmul_push_rhs(zr[slot, unit], 0, unit, transpose=True)

    def stream(sums, step, following):
        slot = lax.rem(step, 2)
        for g, at in enumerate(range(0, cols, GROUP)):
            if at < first_row:
                pair = windows(at, GROUP, step)
            else:
                pair = [zr[slot, unit, at - first_row : at - first_row + GROUP, :] for unit in range(2)]
            for unit in range(2):
                pltpu.matmul_acc_lhs(sums[unit][g], pair[unit], 0 if g == 0 else None)
            if g == 0 and following:
                stage(step + 1)

    def contract(*sums):
        sums = sums[: len(sums) // 2], sums[len(sums) // 2 :]
        for g in range(cols // GROUP):
            for unit in range(2):
                pltpu.matmul_pop(sums[unit][g])
        steps = HALF // STEP_K
        stage(0)

        def advance(step, carry):
            stream(sums, step, True)
            return carry

        lax.fori_loop(0, steps - 1, advance, 0)
        stream(sums, steps - 1, False)
        for g, at in enumerate(range(0, cols, GROUP)):
            acc[at : at + GROUP, :] = pltpu.matmul_pop(sums[0][g]) + pltpu.matmul_pop(sums[1][g])

    pl.run_scoped(contract, *[pltpu.ACC(unit)((GROUP, rows), jnp.float32) for unit in range(2) for _ in range(cols // GROUP)])
    part = lax.axis_index("chan")
    for d, out in enumerate(outs):
        which = part ^ d
        size = out.shape[0]
        out[...] = acc[pl.ds(pl.multiple_of(which * size, 16), size), :].astype(out.dtype)


def peak_kernel(rows, lens, p0, p1, p2, p3, out):
    quarter = p0.shape[0]
    block = lax.axis_index("tm")
    part = lax.axis_index("chan")
    last = rows * lax.axis_size("tm") - WIN
    seg = rows // 2
    start = (block - STEPS) * rows
    f32 = jnp.float32
    score = (p0[...] + p1[...]) + (p2[...].astype(f32) + p3[...].astype(f32))
    shape = (quarter, LANES)
    j = part * quarter + lax.broadcasted_iota(jnp.int32, shape, 0)
    stop = jnp.zeros(shape, jnp.int32)
    for s in range(2 * (STEPS + 1)):
        which = (block - STEPS) * 2 + s
        length = jnp.where(which >= 0, lens[jnp.maximum(which, 0)], 0)
        end = jnp.minimum(s * seg + length, last + 1 - start)
        stop = jnp.where(j >= s * seg, end, stop)
    reach = jnp.where(j < stop, j + EXCL, 2 * (STEPS + 1) * rows)
    lane = lax.broadcasted_iota(jnp.int32, shape, 1)
    for at in range(0, rows, LANES):
        i = lane + (STEPS * rows + at)
        best = jnp.max(jnp.where(i >= reach, score[:, at : at + LANES], MASKED), axis=0, keepdims=True)
        best = jnp.where(best > 0.5 * MASKED, best * (1.0 / WIN), MASKED)
        r = i[:1, :] - STEPS * rows
        own = jnp.where(r < seg, lens[block * 2], seg + lens[block * 2 + 1])
        out[:, at : at + LANES] = jnp.where(r < jnp.minimum(own, last + 1 - block * rows), best, MASKED)


def body(series, lengths):
    chans, rows = series.shape
    parts = lax.axis_size("chan")
    total = (STEPS + 1) * rows
    cols = total - EXCL
    quarter = cols // parts
    b2 = sent(series, "tm", two_on)
    even_side = sent(series, "tm", even_pair)
    odd_side = sent(series, "tm", odd_pair)
    vmem = pl.BlockSpec(memory_space=pltpu.VMEM)
    smem = pl.BlockSpec(memory_space=pltpu.SMEM)
    f32 = jnp.float32
    bf16 = jnp.bfloat16
    room = total + HALF + HALF
    pieces = pl.pallas_call(
        functools.partial(corr_kernel, rows, cols),
        out_shape=[jax.ShapeDtypeStruct((quarter, rows), f32 if d < 2 else bf16) for d in range(parts)],
        in_specs=[pl.BlockSpec(memory_space=pltpu.HBM)] + [vmem] * 3,
        out_specs=[vmem] * parts,
        scratch_shapes=[pltpu.VMEM((chans, rows), f32), pltpu.SemaphoreType.DMA, pltpu.VMEM((room, LANES), f32)]
        + [pltpu.VMEM((ALIGN, room, LANES), f32)]
        + [pltpu.VMEM((room, LANES), f32)] * 4
        + [pltpu.VMEM((2, 2, rows, 2 * LANES), bf16), pltpu.VMEM((cols, rows), f32)],
        compiler_params=pltpu.CompilerParams(vmem_limit_bytes=VMEM_LIMIT),
    )(series, odd_side, b2, even_side)
    got = [pieces[0]] + [sent(pieces[d], "chan", across(d)) for d in range(1, parts)]
    best = pl.pallas_call(
        functools.partial(peak_kernel, rows),
        out_shape=jax.ShapeDtypeStruct((1, rows), f32),
        in_specs=[smem] + [vmem] * parts,
        out_specs=vmem,
        compiler_params=pltpu.CompilerParams(vmem_limit_bytes=SMALL_LIMIT),
    )(lengths, *got)
    peers = [sent(best, "chan", across(d)) for d in range(1, parts)]
    for peer in peers:
        best = jnp.maximum(best, peer)
    return jnp.where(best > 0.5 * MASKED, best, 0.0).reshape(rows)


def solution(mesh):
    return jax.shard_map(
        body,
        mesh=mesh,
        in_specs=(P("chan", "tm"), P()),
        out_specs=P("tm"),
        check_vma=False,
    )
```

```python
import functools

import jax
import jax.numpy as jnp
from jax import lax
from jax.experimental import pallas as pl
from jax.experimental.pallas import tpu as pltpu
from jax.sharding import PartitionSpec as P

WIN = 256
HALF = WIN // 2
STEPS = 2
EPS = 1e-05
MASKED = -1000000000.0
EXCL = WIN // 4
STEP_K = 4
GROUP = 32
UNITS = 2
LANES = 128
ALIGN = 8
VMEM_LIMIT = 16 << 20
SMALL_LIMIT = 8 << 20


def sent(block, axis, target):
    count = lax.axis_size(axis)
    return lax.ppermute(block, axis, [(i, target(i, count)) for i in range(count)])


def two_on(i, count):
    return (i + 2) % count


def even_pair(i, count):
    return i ^ 1


def odd_pair(i, count):
    if i == 0 or i == count - 1:
        return i
    return i + 1 if i % 2 == 1 else i - 1


def across(distance):
    return lambda i, count: i ^ distance


def window_sums(src_m, bufs, span):
    size = 128
    src_v = None
    length = 1
    level = 0
    while length < HALF:
        dst_m, dst_v = bufs[level % 2]

        def step(p, carry, src_m=src_m, src_v=src_v, dst_m=dst_m, dst_v=dst_v, length=length):
            base = pl.multiple_of(p * size, size)
            m0 = src_m[pl.ds(base, size), :]
            m1 = src_m[pl.ds(base + length, size), :]
            gap = m0 - m1
            spread = gap * gap * (0.5 * length)
            if src_v is not None:
                spread = spread + (src_v[pl.ds(base, size), :] + src_v[pl.ds(base + length, size), :])
            dst_m[pl.ds(base, size), :] = (m0 + m1) * 0.5
            dst_v[pl.ds(base, size), :] = spread
            return carry

        lax.fori_loop(0, span // size, step, 0)
        src_m, src_v = dst_m, dst_v
        length *= 2
        level += 1
    return src_m, src_v, bufs[level % 2]


def contract(base, x8, mean_ref, scale_ref, zr, out, fill):
    rows = zr.shape[2]
    size = out.shape[0]
    first_row = STEPS * rows

    def windows(at, step):
        mean = mean_ref[pl.ds(at, GROUP), :]
        scale = scale_ref[pl.ds(at, GROUP), :]
        lag = lax.rem(step, 2) * STEP_K
        start = pl.multiple_of(step // 2 * ALIGN + at, ALIGN)
        z = []
        for k in range(STEP_K):
            x = x8[lag + k, pl.ds(start, GROUP), :]
            z.append(((x - mean) * scale).astype(jnp.bfloat16))
        return jnp.concatenate(z[:2], axis=1), jnp.concatenate(z[2:], axis=1)

    def stage(step):
        if fill:
            for at in range(0, rows, GROUP):
                for unit, z in enumerate(windows(first_row + at, step)):
                    zr[step, unit, at : at + GROUP, :] = z
        for unit in range(UNITS):
            pltpu.matmul_push_rhs(zr[step, unit], 0, unit, transpose=True)

    def run(*sums):
        sums = sums[: len(sums) // UNITS], sums[len(sums) // UNITS :]

        def stream(step, following):
            for g, at in enumerate(range(0, size, GROUP)):
                pair = windows(pl.multiple_of(base + at, GROUP), step)
                for unit in range(UNITS):
                    pltpu.matmul_acc_lhs(sums[unit][g], pair[unit], 0 if g == 0 else None)
                if g == 0 and following:
                    stage(step + 1)

        for g in range(size // GROUP):
            for unit in range(UNITS):
                pltpu.matmul_pop(sums[unit][g])
        steps = HALF // STEP_K
        stage(0)

        def advance(step, carry):
            stream(step, True)
            return carry

        lax.fori_loop(0, steps - 1, advance, 0)
        stream(steps - 1, False)
        for g, at in enumerate(range(0, size, GROUP)):
            both = pltpu.matmul_pop(sums[0][g]) + pltpu.matmul_pop(sums[1][g])
            out[at : at + GROUP, :] = both.astype(out.dtype)

    pl.run_scoped(run, *[pltpu.ACC(unit)((GROUP, rows), jnp.float32) for unit in range(UNITS) for _ in range(size // GROUP)])


def far_kernel(rows, own, odd_side, b2, even_side, out, x8, end_m, end_v, zr, x2, ma, mb, va, vb):
    total = (STEPS + 1) * rows
    span = total + HALF
    odd = lax.rem(lax.axis_index("tm"), 2) == 1
    from_odd, from_even = odd_side[...], even_side[...]
    before = jnp.where(odd, from_even, from_odd)
    after = jnp.where(odd, from_odd, from_even)
    joined = jnp.concatenate([b2[...], before, own[...], after], axis=1)
    both = jnp.concatenate([joined[:, :span], joined[:, HALF : HALF + span]], axis=0)
    for at in range(0, span, LANES):
        x2[at : at + LANES, :] = both[:, at : at + LANES].T

    src_m, src_v, _ = window_sums(x2, [(ma, va), (mb, vb)], span)
    for at in range(0, total, LANES):
        m0 = src_m[at : at + LANES, :]
        v0 = src_v[at : at + LANES, :]
        m1 = pltpu.roll(m0, LANES // 2, 1)
        v1 = pltpu.roll(v0, LANES // 2, 1)
        gap = m0 - m1
        var = (v0 + v1 + gap * gap * (0.5 * HALF)) * (1.0 / WIN)
        end_m[at : at + LANES, :] = (m0 + m1) * 0.5
        end_v[at : at + LANES, :] = lax.rsqrt(var + EPS)

    for s in range(ALIGN):
        for at in range(0, span, LANES):
            x8[s, at : at + LANES, :] = x2[at + s : at + s + LANES, :]

    base = (1 - lax.axis_index("chan") // 2) * out.shape[0]
    contract(base, x8, end_m, end_v, zr, out, True)


def near_kernel(x8, end_m, end_v, zr, out):
    base = lax.axis_index("chan") // 2 * out.shape[0]
    contract(base, x8, end_m, end_v, zr, out, False)


def peak_kernel(rows, lens, p0, p1, p2, p3, out):
    quarter = p0.shape[0]
    block = lax.axis_index("tm")
    part = lax.axis_index("chan") // 2
    last = rows * lax.axis_size("tm") - WIN
    seg = rows // 2
    start = (block - STEPS) * rows
    f32 = jnp.float32
    score = (p0[...] + p1[...]) + (p2[...].astype(f32) + p3[...].astype(f32))
    shape = (quarter, LANES)
    j = part * quarter + lax.broadcasted_iota(jnp.int32, shape, 0)
    stop = jnp.zeros(shape, jnp.int32)
    for s in range(2 * (STEPS + 1)):
        which = (block - STEPS) * 2 + s
        length = jnp.where(which >= 0, lens[jnp.maximum(which, 0)], 0)
        end = jnp.minimum(s * seg + length, last + 1 - start)
        stop = jnp.where(j >= s * seg, end, stop)
    reach = jnp.where(j < stop, j + EXCL, 2 * (STEPS + 1) * rows)
    lane = lax.broadcasted_iota(jnp.int32, shape, 1)
    for at in range(0, rows, LANES):
        i = lane + (STEPS * rows + at)
        best = jnp.max(jnp.where(i >= reach, score[:, at : at + LANES], MASKED), axis=0, keepdims=True)
        best = jnp.where(best > 0.5 * MASKED, best * (1.0 / WIN), MASKED)
        r = i[:1, :] - STEPS * rows
        own = jnp.where(r < seg, lens[block * 2], seg + lens[block * 2 + 1])
        out[:, at : at + LANES] = jnp.where(r < jnp.minimum(own, last + 1 - block * rows), best, MASKED)


def body(series, lengths):
    chans, rows = series.shape
    total = (STEPS + 1) * rows
    cols = total - EXCL
    side = cols // 2
    even_side = sent(series, "tm", even_pair)
    b2 = sent(series, "tm", two_on)
    odd_side = sent(series, "tm", odd_pair)
    vmem = pl.BlockSpec(memory_space=pltpu.VMEM)
    smem = pl.BlockSpec(memory_space=pltpu.SMEM)
    f32 = jnp.float32
    bf16 = jnp.bfloat16
    room = total + HALF + HALF
    tall = jax.ShapeDtypeStruct((room, LANES), f32)
    far, *shared = pl.pallas_call(
        functools.partial(far_kernel, rows),
        out_shape=[
            jax.ShapeDtypeStruct((side, rows), bf16),
            jax.ShapeDtypeStruct((ALIGN, room, LANES), f32),
            tall,
            tall,
            jax.ShapeDtypeStruct((HALF // STEP_K, UNITS, rows, 2 * LANES), bf16),
        ],
        in_specs=[vmem] * 4,
        out_specs=[vmem] * 5,
        scratch_shapes=[pltpu.VMEM((room, LANES), f32)] * 5,
        compiler_params=pltpu.CompilerParams(vmem_limit_bytes=VMEM_LIMIT),
    )(series, odd_side, b2, even_side)
    far_got = sent(far, "chan", across(2))
    near = pl.pallas_call(
        near_kernel,
        out_shape=jax.ShapeDtypeStruct((side, rows), f32),
        in_specs=[vmem] * 4,
        out_specs=vmem,
        compiler_params=pltpu.CompilerParams(vmem_limit_bytes=SMALL_LIMIT),
    )(*shared)
    near_peer = sent(near, "chan", across(1))
    far_peer = sent(far_got, "chan", across(1))
    best = pl.pallas_call(
        functools.partial(peak_kernel, rows),
        out_shape=jax.ShapeDtypeStruct((1, rows), f32),
        in_specs=[smem] + [vmem] * 4,
        out_specs=vmem,
        compiler_params=pltpu.CompilerParams(vmem_limit_bytes=SMALL_LIMIT),
    )(lengths, near, near_peer, far_got, far_peer)
    best = jnp.maximum(best, sent(best, "chan", across(2)))
    return jnp.where(best > 0.5 * MASKED, best, 0.0).reshape(rows)


def solution(mesh):
    return jax.shard_map(
        body,
        mesh=mesh,
        in_specs=(P("chan", "tm"), P()),
        out_specs=P("tm"),
        check_vma=False,
    )
```

```python
import functools

import jax
import jax.numpy as jnp
from jax import lax
from jax.experimental import pallas as pl
from jax.experimental.pallas import tpu as pltpu
from jax.sharding import PartitionSpec as P

WIN = 256
HALF = WIN // 2
STEPS = 2
EPS = 1e-05
MASKED = -1000000000.0
EXCL = WIN // 4
STEP_K = 4
GROUP = 32
UNITS = 2
LANES = 128
ALIGN = 8
VMEM_LIMIT = 16 << 20
SMALL_LIMIT = 8 << 20


def sent(block, axis, target):
    count = lax.axis_size(axis)
    return lax.ppermute(block, axis, [(i, target(i, count)) for i in range(count)])


LINE = 4


def first_step(i, count):
    return (i + (2, 2, -1, 1)[i % LINE]) % count


def second_step(i, count):
    if i in (0, count - 1):
        return i
    if i == count - 2:
        return 1
    return i + (-1, 1, 2, 2)[i % LINE]


def third_step(i, count):
    return i ^ 1


def across(distance):
    return lambda i, count: i ^ distance


def window_sums(src_m, bufs, span):
    size = 128
    src_v = None
    length = 1
    level = 0
    while length < HALF:
        dst_m, dst_v = bufs[level % 2]

        def step(p, carry, src_m=src_m, src_v=src_v, dst_m=dst_m, dst_v=dst_v, length=length):
            base = pl.multiple_of(p * size, size)
            m0 = src_m[pl.ds(base, size), :]
            m1 = src_m[pl.ds(base + length, size), :]
            gap = m0 - m1
            spread = gap * gap * (0.5 * length)
            if src_v is not None:
                spread = spread + (src_v[pl.ds(base, size), :] + src_v[pl.ds(base + length, size), :])
            dst_m[pl.ds(base, size), :] = (m0 + m1) * 0.5
            dst_v[pl.ds(base, size), :] = spread
            return carry

        lax.fori_loop(0, span // size, step, 0)
        src_m, src_v = dst_m, dst_v
        length *= 2
        level += 1
    return src_m, src_v, bufs[level % 2]


def contract(base, x8, mean_ref, scale_ref, zr, out, fill):
    rows = zr.shape[2]
    size = out.shape[0]
    first_row = STEPS * rows

    def windows(at, step):
        mean = mean_ref[pl.ds(at, GROUP), :]
        scale = scale_ref[pl.ds(at, GROUP), :]
        lag = lax.rem(step, 2) * STEP_K
        start = pl.multiple_of(step // 2 * ALIGN + at, ALIGN)
        z = []
        for k in range(STEP_K):
            x = x8[lag + k, pl.ds(start, GROUP), :]
            z.append(((x - mean) * scale).astype(jnp.bfloat16))
        return jnp.concatenate(z[:2], axis=1), jnp.concatenate(z[2:], axis=1)

    def stage(step):
        if fill:
            for at in range(0, rows, GROUP):
                for unit, z in enumerate(windows(first_row + at, step)):
                    zr[step, unit, at : at + GROUP, :] = z
        for unit in range(UNITS):
            pltpu.matmul_push_rhs(zr[step, unit], 0, unit, transpose=True)

    def run(*sums):
        sums = sums[: len(sums) // UNITS], sums[len(sums) // UNITS :]

        def stream(step, following):
            for g, at in enumerate(range(0, size, GROUP)):
                pair = windows(pl.multiple_of(base + at, GROUP), step)
                for unit in range(UNITS):
                    pltpu.matmul_acc_lhs(sums[unit][g], pair[unit], 0 if g == 0 else None)
                if g == 0 and following:
                    stage(step + 1)

        for g in range(size // GROUP):
            for unit in range(UNITS):
                pltpu.matmul_pop(sums[unit][g])
        steps = HALF // STEP_K
        stage(0)

        def advance(step, carry):
            stream(step, True)
            return carry

        lax.fori_loop(0, steps - 1, advance, 0)
        stream(steps - 1, False)
        for g, at in enumerate(range(0, size, GROUP)):
            both = pltpu.matmul_pop(sums[0][g]) + pltpu.matmul_pop(sums[1][g])
            out[at : at + GROUP, :] = both.astype(out.dtype)

    pl.run_scoped(run, *[pltpu.ACC(unit)((GROUP, rows), jnp.float32) for unit in range(UNITS) for _ in range(size // GROUP)])


def far_kernel(rows, own, from_first, from_third, from_second, out, x8, end_m, end_v, zr, x2, ma, mb, va, vb):
    total = (STEPS + 1) * rows
    span = total + HALF
    place = lax.rem(lax.axis_index("tm"), LINE)
    first, second, third = from_first[...], from_second[...], from_third[...]
    earlier = jnp.where(place < 2, second, first)
    odd = lax.rem(place, 2) == 1
    before = jnp.where(odd, third, jnp.where(place == 0, first, second))
    after = jnp.where(odd, jnp.where(place == 1, first, second), third)
    joined = jnp.concatenate([earlier, before, own[...], after], axis=1)
    both = jnp.concatenate([joined[:, :span], joined[:, HALF : HALF + span]], axis=0)
    for at in range(0, span, LANES):
        x2[at : at + LANES, :] = both[:, at : at + LANES].T

    src_m, src_v, _ = window_sums(x2, [(ma, va), (mb, vb)], span)
    for at in range(0, total, LANES):
        m0 = src_m[at : at + LANES, :]
        v0 = src_v[at : at + LANES, :]
        m1 = pltpu.roll(m0, LANES // 2, 1)
        v1 = pltpu.roll(v0, LANES // 2, 1)
        gap = m0 - m1
        var = (v0 + v1 + gap * gap * (0.5 * HALF)) * (1.0 / WIN)
        end_m[at : at + LANES, :] = (m0 + m1) * 0.5
        end_v[at : at + LANES, :] = lax.rsqrt(var + EPS)

    for s in range(ALIGN):
        for at in range(0, span, LANES):
            x8[s, at : at + LANES, :] = x2[at + s : at + s + LANES, :]

    base = (1 - lax.axis_index("chan") // 2) * out.shape[0]
    contract(base, x8, end_m, end_v, zr, out, True)


def near_kernel(x8, end_m, end_v, zr, out):
    base = lax.axis_index("chan") // 2 * out.shape[0]
    contract(base, x8, end_m, end_v, zr, out, False)


def peak_kernel(rows, lens, p0, p1, p2, p3, out):
    quarter = p0.shape[0]
    block = lax.axis_index("tm")
    part = lax.axis_index("chan") // 2
    last = rows * lax.axis_size("tm") - WIN
    seg = rows // 2
    start = (block - STEPS) * rows
    f32 = jnp.float32
    score = (p0[...] + p1[...]) + (p2[...].astype(f32) + p3[...].astype(f32))
    shape = (quarter, LANES)
    j = part * quarter + lax.broadcasted_iota(jnp.int32, shape, 0)
    stop = jnp.zeros(shape, jnp.int32)
    for s in range(2 * (STEPS + 1)):
        which = (block - STEPS) * 2 + s
        length = jnp.where(which >= 0, lens[jnp.maximum(which, 0)], 0)
        end = jnp.minimum(s * seg + length, last + 1 - start)
        stop = jnp.where(j >= s * seg, end, stop)
    reach = jnp.where(j < stop, j + EXCL, 2 * (STEPS + 1) * rows)
    lane = lax.broadcasted_iota(jnp.int32, shape, 1)
    for at in range(0, rows, LANES):
        i = lane + (STEPS * rows + at)
        best = jnp.max(jnp.where(i >= reach, score[:, at : at + LANES], MASKED), axis=0, keepdims=True)
        best = jnp.where(best > 0.5 * MASKED, best * (1.0 / WIN), MASKED)
        r = i[:1, :] - STEPS * rows
        own = jnp.where(r < seg, lens[block * 2], seg + lens[block * 2 + 1])
        out[:, at : at + LANES] = jnp.where(r < jnp.minimum(own, last + 1 - block * rows), best, MASKED)


def body(series, lengths):
    chans, rows = series.shape
    total = (STEPS + 1) * rows
    cols = total - EXCL
    side = cols // 2
    own = jnp.maximum(series, jnp.finfo(series.dtype).min)
    from_first = sent(series, "tm", first_step)
    from_second = sent(series, "tm", second_step)
    from_third = sent(series, "tm", third_step)
    vmem = pl.BlockSpec(memory_space=pltpu.VMEM)
    smem = pl.BlockSpec(memory_space=pltpu.SMEM)
    f32 = jnp.float32
    bf16 = jnp.bfloat16
    room = total + HALF + HALF
    tall = jax.ShapeDtypeStruct((room, LANES), f32)
    far, *shared = pl.pallas_call(
        functools.partial(far_kernel, rows),
        out_shape=[
            jax.ShapeDtypeStruct((side, rows), bf16),
            jax.ShapeDtypeStruct((ALIGN, room, LANES), f32),
            tall,
            tall,
            jax.ShapeDtypeStruct((HALF // STEP_K, UNITS, rows, 2 * LANES), bf16),
        ],
        in_specs=[vmem] * 4,
        out_specs=[vmem] * 5,
        scratch_shapes=[pltpu.VMEM((room, LANES), f32)] * 5,
        compiler_params=pltpu.CompilerParams(vmem_limit_bytes=VMEM_LIMIT),
    )(own, from_first, from_third, from_second)
    far_got = sent(far, "chan", across(2))
    near = pl.pallas_call(
        near_kernel,
        out_shape=jax.ShapeDtypeStruct((side, rows), f32),
        in_specs=[vmem] * 4,
        out_specs=vmem,
        compiler_params=pltpu.CompilerParams(vmem_limit_bytes=SMALL_LIMIT),
    )(*shared)
    near_peer = sent(near, "chan", across(1))
    far_peer = sent(far_got, "chan", across(1))
    best = pl.pallas_call(
        functools.partial(peak_kernel, rows),
        out_shape=jax.ShapeDtypeStruct((1, rows), f32),
        in_specs=[smem] + [vmem] * 4,
        out_specs=vmem,
        compiler_params=pltpu.CompilerParams(vmem_limit_bytes=SMALL_LIMIT),
    )(lengths, near, near_peer, far_got, far_peer)
    best = jnp.maximum(best, sent(best, "chan", across(2)))
    return jnp.where(best > 0.5 * MASKED, best, 0.0).reshape(rows)


def solution(mesh):
    return jax.shard_map(
        body,
        mesh=mesh,
        in_specs=(P("chan", "tm"), P()),
        out_specs=P("tm"),
        check_vma=False,
    )
```

```python
import functools

import jax
import jax.numpy as jnp
from jax import lax
from jax.experimental import pallas as pl
from jax.experimental.pallas import tpu as pltpu
from jax.sharding import PartitionSpec as P

WIN = 256
HALF = WIN // 2
STEPS = 2
EPS = 1e-05
MASKED = -1000000000.0
EXCL = WIN // 4
STEP_K = 4
GROUP = 32
UNITS = 2
LANES = 128
ALIGN = 8
VMEM_LIMIT = 16 << 20
SMALL_LIMIT = 8 << 20


def sent(block, axis, target):
    count = lax.axis_size(axis)
    return lax.ppermute(block, axis, [(i, target(i, count)) for i in range(count)])


LINE = 4


def first_step(i, count):
    return (i + (2, 2, -1, 1)[i % LINE]) % count


def second_step(i, count):
    return (i + (-1, 1, 2, 2)[i % LINE]) % count


def third_step(i, count):
    return i ^ 1


def across(distance):
    return lambda i, count: i ^ distance


def window_sums(src_m, bufs, span):
    size = 128
    src_v = None
    length = 1
    level = 0
    while length < HALF:
        dst_m, dst_v = bufs[level % 2]

        def step(p, carry, src_m=src_m, src_v=src_v, dst_m=dst_m, dst_v=dst_v, length=length):
            base = pl.multiple_of(p * size, size)
            m0 = src_m[pl.ds(base, size), :]
            m1 = src_m[pl.ds(base + length, size), :]
            gap = m0 - m1
            spread = gap * gap * (0.5 * length)
            if src_v is not None:
                spread = spread + (src_v[pl.ds(base, size), :] + src_v[pl.ds(base + length, size), :])
            dst_m[pl.ds(base, size), :] = (m0 + m1) * 0.5
            dst_v[pl.ds(base, size), :] = spread
            return carry

        lax.fori_loop(0, span // size, step, 0)
        src_m, src_v = dst_m, dst_v
        length *= 2
        level += 1
    return src_m, src_v, bufs[level % 2]


def contract(base, x8, mean_ref, scale_ref, zr, out, fill):
    rows = zr.shape[2]
    size = out.shape[0]
    first_row = STEPS * rows

    def windows(at, step):
        mean = mean_ref[pl.ds(at, GROUP), :]
        scale = scale_ref[pl.ds(at, GROUP), :]
        lag = lax.rem(step, 2) * STEP_K
        start = pl.multiple_of(step // 2 * ALIGN + at, ALIGN)
        z = []
        for k in range(STEP_K):
            x = x8[lag + k, pl.ds(start, GROUP), :]
            z.append(((x - mean) * scale).astype(jnp.bfloat16))
        return jnp.concatenate(z[:2], axis=1), jnp.concatenate(z[2:], axis=1)

    def stage(step):
        if fill:
            for at in range(0, rows, GROUP):
                for unit, z in enumerate(windows(first_row + at, step)):
                    zr[step, unit, at : at + GROUP, :] = z
        for unit in range(UNITS):
            pltpu.matmul_push_rhs(zr[step, unit], 0, unit, transpose=True)

    def run(*sums):
        sums = sums[: len(sums) // UNITS], sums[len(sums) // UNITS :]

        def stream(step, following):
            for g, at in enumerate(range(0, size, GROUP)):
                pair = windows(pl.multiple_of(base + at, GROUP), step)
                for unit in range(UNITS):
                    pltpu.matmul_acc_lhs(sums[unit][g], pair[unit], 0 if g == 0 else None)
                if g == 0 and following:
                    stage(step + 1)

        for g in range(size // GROUP):
            for unit in range(UNITS):
                pltpu.matmul_pop(sums[unit][g])
        steps = HALF // STEP_K
        stage(0)

        def advance(step, carry):
            stream(step, True)
            return carry

        lax.fori_loop(0, steps - 1, advance, 0)
        stream(steps - 1, False)
        for g, at in enumerate(range(0, size, GROUP)):
            both = pltpu.matmul_pop(sums[0][g]) + pltpu.matmul_pop(sums[1][g])
            out[at : at + GROUP, :] = both.astype(out.dtype)

    pl.run_scoped(run, *[pltpu.ACC(unit)((GROUP, rows), jnp.float32) for unit in range(UNITS) for _ in range(size // GROUP)])


def far_kernel(rows, own, from_first, from_third, from_second, out, x8, end_m, end_v, zr, x2, ma, mb, va, vb):
    total = (STEPS + 1) * rows
    span = total + HALF
    place = lax.rem(lax.axis_index("tm"), LINE)
    first, second, third = from_first[...], from_second[...], from_third[...]
    earlier = jnp.where(place < 2, second, first)
    odd = lax.rem(place, 2) == 1
    before = jnp.where(odd, third, jnp.where(place == 0, first, second))
    after = jnp.where(odd, jnp.where(place == 1, first, second), third)
    joined = jnp.concatenate([earlier, before, own[...], after], axis=1)
    both = jnp.concatenate([joined[:, :span], joined[:, HALF : HALF + span]], axis=0)
    for at in range(0, span, LANES):
        x2[at : at + LANES, :] = both[:, at : at + LANES].T

    src_m, src_v, _ = window_sums(x2, [(ma, va), (mb, vb)], span)
    for at in range(0, total, LANES):
        m0 = src_m[at : at + LANES, :]
        v0 = src_v[at : at + LANES, :]
        m1 = pltpu.roll(m0, LANES // 2, 1)
        v1 = pltpu.roll(v0, LANES // 2, 1)
        gap = m0 - m1
        var = (v0 + v1 + gap * gap * (0.5 * HALF)) * (1.0 / WIN)
        end_m[at : at + LANES, :] = (m0 + m1) * 0.5
        end_v[at : at + LANES, :] = lax.rsqrt(var + EPS)

    for s in range(ALIGN):
        for at in range(0, span, LANES):
            x8[s, at : at + LANES, :] = x2[at + s : at + s + LANES, :]

    base = (1 - lax.axis_index("chan") // 2) * out.shape[0]
    contract(base, x8, end_m, end_v, zr, out, True)


def near_kernel(x8, end_m, end_v, zr, out):
    base = lax.axis_index("chan") // 2 * out.shape[0]
    contract(base, x8, end_m, end_v, zr, out, False)


def peak_kernel(rows, lens, p0, p1, p2, p3, out):
    quarter = p0.shape[0]
    block = lax.axis_index("tm")
    part = lax.axis_index("chan") // 2
    last = rows * lax.axis_size("tm") - WIN
    seg = rows // 2
    start = (block - STEPS) * rows
    f32 = jnp.float32
    score = (p0[...] + p1[...]) + (p2[...].astype(f32) + p3[...].astype(f32))
    shape = (quarter, LANES)
    j = part * quarter + lax.broadcasted_iota(jnp.int32, shape, 0)
    stop = jnp.zeros(shape, jnp.int32)
    for s in range(2 * (STEPS + 1)):
        which = (block - STEPS) * 2 + s
        length = jnp.where(which >= 0, lens[jnp.maximum(which, 0)], 0)
        end = jnp.minimum(s * seg + length, last + 1 - start)
        stop = jnp.where(j >= s * seg, end, stop)
    reach = jnp.where(j < stop, j + EXCL, 2 * (STEPS + 1) * rows)
    lane = lax.broadcasted_iota(jnp.int32, shape, 1)
    for at in range(0, rows, LANES):
        i = lane + (STEPS * rows + at)
        best = jnp.max(jnp.where(i >= reach, score[:, at : at + LANES], MASKED), axis=0, keepdims=True)
        best = jnp.where(best > 0.5 * MASKED, best * (1.0 / WIN), MASKED)
        r = i[:1, :] - STEPS * rows
        own = jnp.where(r < seg, lens[block * 2], seg + lens[block * 2 + 1])
        out[:, at : at + LANES] = jnp.where(r < jnp.minimum(own, last + 1 - block * rows), best, MASKED)


def body(series, lengths):
    chans, rows = series.shape
    total = (STEPS + 1) * rows
    cols = total - EXCL
    side = cols // 2
    own = jnp.maximum(series, jnp.finfo(series.dtype).min)
    from_first = sent(series, "tm", first_step)
    from_second = sent(series, "tm", second_step)
    from_third = sent(series, "tm", third_step)
    vmem = pl.BlockSpec(memory_space=pltpu.VMEM)
    smem = pl.BlockSpec(memory_space=pltpu.SMEM)
    f32 = jnp.float32
    bf16 = jnp.bfloat16
    room = total + HALF + HALF
    tall = jax.ShapeDtypeStruct((room, LANES), f32)
    far, *shared = pl.pallas_call(
        functools.partial(far_kernel, rows),
        out_shape=[
            jax.ShapeDtypeStruct((side, rows), bf16),
            jax.ShapeDtypeStruct((ALIGN, room, LANES), f32),
            tall,
            tall,
            jax.ShapeDtypeStruct((HALF // STEP_K, UNITS, rows, 2 * LANES), bf16),
        ],
        in_specs=[vmem] * 4,
        out_specs=[vmem] * 5,
        scratch_shapes=[pltpu.VMEM((room, LANES), f32)] * 5,
        compiler_params=pltpu.CompilerParams(vmem_limit_bytes=VMEM_LIMIT),
    )(own, from_first, from_third, from_second)
    far_got = sent(far, "chan", across(2))
    near = pl.pallas_call(
        near_kernel,
        out_shape=jax.ShapeDtypeStruct((side, rows), f32),
        in_specs=[vmem] * 4,
        out_specs=vmem,
        compiler_params=pltpu.CompilerParams(vmem_limit_bytes=SMALL_LIMIT),
    )(*shared)
    near_peer = sent(near, "chan", across(1))
    far_peer = sent(far_got, "chan", across(1))
    best = pl.pallas_call(
        functools.partial(peak_kernel, rows),
        out_shape=jax.ShapeDtypeStruct((1, rows), f32),
        in_specs=[smem] + [vmem] * 4,
        out_specs=vmem,
        compiler_params=pltpu.CompilerParams(vmem_limit_bytes=SMALL_LIMIT),
    )(lengths, near, near_peer, far_got, far_peer)
    best = jnp.maximum(best, sent(best, "chan", across(2)))
    return jnp.where(best > 0.5 * MASKED, best, 0.0).reshape(rows)


def solution(mesh):
    return jax.shard_map(
        body,
        mesh=mesh,
        in_specs=(P("chan", "tm"), P()),
        out_specs=P("tm"),
        check_vma=False,
    )
```

```python
import functools

import jax
import jax.numpy as jnp
from jax import lax
from jax.experimental import pallas as pl
from jax.experimental.pallas import tpu as pltpu
from jax.sharding import PartitionSpec as P

WIN = 256
HALF = WIN // 2
STEPS = 2
EPS = 1e-05
MASKED = -1000000000.0
EXCL = WIN // 4
STEP_K = 4
GROUP = 32
UNITS = 2
LANES = 128
ALIGN = 8
SMALL_LIMIT = 8 << 20


def sent(block, axis, target):
    count = lax.axis_size(axis)
    return lax.ppermute(block, axis, [(i, target(i, count)) for i in range(count)])


LINE = 4


def first_step(i, count):
    return (i + (2, 2, -1, 1)[i % LINE]) % count


def second_step(i, count):
    if i == 0:
        return 1
    if i == count - 2:
        return count - 1
    if i == count - 1:
        return 0
    return i + (-1, 1, 2, 2)[i % LINE]


def third_step(i, count):
    return i ^ 1


def across(distance):
    return lambda i, count: i ^ distance


def window_sums(src_m, bufs, span):
    size = 128
    src_v = None
    length = 1
    level = 0
    while length < HALF:
        dst_m, dst_v = bufs[level % 2]

        def step(p, carry, src_m=src_m, src_v=src_v, dst_m=dst_m, dst_v=dst_v, length=length):
            base = pl.multiple_of(p * size, size)
            m0 = src_m[pl.ds(base, size), :]
            m1 = src_m[pl.ds(base + length, size), :]
            gap = m0 - m1
            spread = gap * gap * (0.5 * length)
            if src_v is not None:
                spread = spread + (src_v[pl.ds(base, size), :] + src_v[pl.ds(base + length, size), :])
            dst_m[pl.ds(base, size), :] = (m0 + m1) * 0.5
            dst_v[pl.ds(base, size), :] = spread
            return carry

        lax.fori_loop(0, span // size, step, 0)
        src_m, src_v = dst_m, dst_v
        length *= 2
        level += 1
    return src_m, src_v, bufs[level % 2]


def contract(base, x8, mean_ref, scale_ref, zr, out, fill):
    rows = zr.shape[2]
    size = out.shape[0]
    first_row = STEPS * rows

    def windows(at, step):
        mean = mean_ref[pl.ds(at, GROUP), :]
        scale = scale_ref[pl.ds(at, GROUP), :]
        lag = lax.rem(step, 2) * STEP_K
        start = pl.multiple_of(step // 2 * ALIGN + at, ALIGN)
        z = []
        for k in range(STEP_K):
            x = x8[lag + k, pl.ds(start, GROUP), :]
            z.append(((x - mean) * scale).astype(jnp.bfloat16))
        return jnp.concatenate(z[:2], axis=1), jnp.concatenate(z[2:], axis=1)

    def stage(step):
        if fill:
            for at in range(0, rows, GROUP):
                for unit, z in enumerate(windows(first_row + at, step)):
                    zr[step, unit, at : at + GROUP, :] = z
        for unit in range(UNITS):
            pltpu.matmul_push_rhs(zr[step, unit], 0, unit, transpose=True)

    def run(*sums):
        sums = sums[: len(sums) // UNITS], sums[len(sums) // UNITS :]

        def stream(step, following):
            for g, at in enumerate(range(0, size, GROUP)):
                pair = windows(pl.multiple_of(base + at, GROUP), step)
                for unit in range(UNITS):
                    pltpu.matmul_acc_lhs(sums[unit][g], pair[unit], 0 if g == 0 else None)
                if g == 0 and following:
                    stage(step + 1)

        for g in range(size // GROUP):
            for unit in range(UNITS):
                pltpu.matmul_pop(sums[unit][g])
        steps = HALF // STEP_K
        stage(0)

        def advance(step, carry):
            stream(step, True)
            return carry

        lax.fori_loop(0, steps - 1, advance, 0)
        stream(steps - 1, False)
        for g, at in enumerate(range(0, size, GROUP)):
            both = pltpu.matmul_pop(sums[0][g]) + pltpu.matmul_pop(sums[1][g])
            out[at : at + GROUP, :] = both.astype(out.dtype)

    pl.run_scoped(run, *[pltpu.ACC(unit)((GROUP, rows), jnp.float32) for unit in range(UNITS) for _ in range(size // GROUP)])


def prepare(at_block, left, right, x8, end_m, end_v, work):
    x2, ma, mb, va, vb = work
    rows = left.shape[1]
    span = rows + HALF
    first = at_block * rows
    joined = jnp.concatenate([left, right], axis=1)
    both = jnp.concatenate([joined[:, :span], joined[:, HALF : HALF + span]], axis=0)
    for at in range(0, span, LANES):
        x2[at : at + LANES, :] = both[:, at : at + LANES].T
    src_m, src_v, _ = window_sums(x2, [(ma, va), (mb, vb)], span)
    for at in range(0, rows, LANES):
        m0 = src_m[at : at + LANES, :]
        v0 = src_v[at : at + LANES, :]
        m1 = pltpu.roll(m0, LANES // 2, 1)
        v1 = pltpu.roll(v0, LANES // 2, 1)
        gap = m0 - m1
        var = (v0 + v1 + gap * gap * (0.5 * HALF)) * (1.0 / WIN)
        end_m[first + at : first + at + LANES, :] = (m0 + m1) * 0.5
        end_v[first + at : first + at + LANES, :] = lax.rsqrt(var + EPS)
    held = span if at_block == STEPS else rows
    for s in range(ALIGN):
        for at in range(0, held, LANES):
            x8[s, first + at : first + at + LANES, :] = x2[at + s : at + s + LANES, :]


def neighbours(place, from_first, from_second, from_third):
    second = from_first if from_second is None else from_second
    earlier = jnp.where(place < 2, second, from_first)
    odd = lax.rem(place, 2) == 1
    before = jnp.where(odd, from_third, jnp.where(place == 0, from_first, second))
    after = jnp.where(odd, jnp.where(place == 1, from_first, second), from_third)
    return earlier, before, after


def early_kernel(own, from_first, from_third, x8, end_m, end_v, *work):
    place = lax.rem(lax.axis_index("tm"), LINE)

    @pl.when(place < 2)
    def _():
        _, before, after = neighbours(place, from_first[...], None, from_third[...])
        prepare(1, before, own[...], x8, end_m, end_v, work)
        prepare(2, own[...], after, x8, end_m, end_v, work)


def far_kernel(own, from_first, from_third, from_second, _x8, _m, _v, out, x8, end_m, end_v, zr, *work):
    place = lax.rem(lax.axis_index("tm"), LINE)
    earlier, before, after = neighbours(place, from_first[...], from_second[...], from_third[...])
    prepare(0, earlier, before, x8, end_m, end_v, work)

    @pl.when(place >= 2)
    def _():
        prepare(1, before, own[...], x8, end_m, end_v, work)
        prepare(2, own[...], after, x8, end_m, end_v, work)

    base = (1 - lax.axis_index("chan") // 2) * out.shape[0]
    contract(base, x8, end_m, end_v, zr, out, True)


def near_kernel(x8, end_m, end_v, zr, out):
    base = lax.axis_index("chan") // 2 * out.shape[0]
    contract(base, x8, end_m, end_v, zr, out, False)


def peak_kernel(rows, lens, p0, p1, p2, p3, out):
    quarter = p0.shape[0]
    block = lax.axis_index("tm")
    part = lax.axis_index("chan") // 2
    last = rows * lax.axis_size("tm") - WIN
    seg = rows // 2
    start = (block - STEPS) * rows
    f32 = jnp.float32
    score = (p0[...] + p1[...]) + (p2[...].astype(f32) + p3[...].astype(f32))
    shape = (quarter, LANES)
    j = part * quarter + lax.broadcasted_iota(jnp.int32, shape, 0)
    stop = jnp.zeros(shape, jnp.int32)
    for s in range(2 * (STEPS + 1)):
        which = (block - STEPS) * 2 + s
        length = jnp.where(which >= 0, lens[jnp.maximum(which, 0)], 0)
        end = jnp.minimum(s * seg + length, last + 1 - start)
        stop = jnp.where(j >= s * seg, end, stop)
    reach = jnp.where(j < stop, j + EXCL, 2 * (STEPS + 1) * rows)
    lane = lax.broadcasted_iota(jnp.int32, shape, 1)
    for at in range(0, rows, LANES):
        i = lane + (STEPS * rows + at)
        best = jnp.max(jnp.where(i >= reach, score[:, at : at + LANES], MASKED), axis=0, keepdims=True)
        best = jnp.where(best > 0.5 * MASKED, best * (1.0 / WIN), MASKED)
        r = i[:1, :] - STEPS * rows
        own = jnp.where(r < seg, lens[block * 2], seg + lens[block * 2 + 1])
        out[:, at : at + LANES] = jnp.where(r < jnp.minimum(own, last + 1 - block * rows), best, MASKED)


def body(series, lengths):
    chans, rows = series.shape
    total = (STEPS + 1) * rows
    cols = total - EXCL
    side = cols // 2
    own = jnp.maximum(series, jnp.finfo(series.dtype).min)
    from_first = sent(series, "tm", first_step)
    from_second = sent(series, "tm", second_step)
    from_third = sent(series, "tm", third_step)
    vmem = pl.BlockSpec(memory_space=pltpu.VMEM)
    smem = pl.BlockSpec(memory_space=pltpu.SMEM)
    f32 = jnp.float32
    bf16 = jnp.bfloat16
    room = total + HALF + HALF
    tall = jax.ShapeDtypeStruct((room, LANES), f32)
    shifted = jax.ShapeDtypeStruct((ALIGN, room, LANES), f32)
    work = [pltpu.VMEM((rows + 2 * HALF, LANES), f32)] * 5
    early = pl.pallas_call(
        early_kernel,
        out_shape=[shifted, tall, tall],
        in_specs=[vmem] * 3,
        out_specs=[vmem] * 3,
        scratch_shapes=work,
        compiler_params=pltpu.CompilerParams(vmem_limit_bytes=SMALL_LIMIT),
    )(own, from_first, from_third)
    far, *shared = pl.pallas_call(
        far_kernel,
        out_shape=[
            jax.ShapeDtypeStruct((side, rows), bf16),
            shifted,
            tall,
            tall,
            jax.ShapeDtypeStruct((HALF // STEP_K, UNITS, rows, 2 * LANES), bf16),
        ],
        in_specs=[vmem] * 7,
        out_specs=[vmem] * 5,
        input_output_aliases={4: 1, 5: 2, 6: 3},
        scratch_shapes=work,
        compiler_params=pltpu.CompilerParams(vmem_limit_bytes=SMALL_LIMIT),
    )(own, from_first, from_third, from_second, *early)
    far_got = sent(far, "chan", across(2))
    near = pl.pallas_call(
        near_kernel,
        out_shape=jax.ShapeDtypeStruct((side, rows), f32),
        in_specs=[vmem] * 4,
        out_specs=vmem,
        compiler_params=pltpu.CompilerParams(vmem_limit_bytes=SMALL_LIMIT),
    )(*shared)
    near_peer = sent(near, "chan", across(1))
    far_peer = sent(far_got, "chan", across(1))
    best = pl.pallas_call(
        functools.partial(peak_kernel, rows),
        out_shape=jax.ShapeDtypeStruct((1, rows), f32),
        in_specs=[smem] + [vmem] * 4,
        out_specs=vmem,
        compiler_params=pltpu.CompilerParams(vmem_limit_bytes=SMALL_LIMIT),
    )(lengths, near, near_peer, far_got, far_peer)
    best = jnp.maximum(best, sent(best, "chan", across(2)))
    return jnp.where(best > 0.5 * MASKED, best, 0.0).reshape(rows)


def solution(mesh):
    return jax.shard_map(
        body,
        mesh=mesh,
        in_specs=(P("chan", "tm"), P()),
        out_specs=P("tm"),
        check_vma=False,
    )
```

```python
import functools

import jax
import jax.numpy as jnp
from jax import lax
from jax.experimental import pallas as pl
from jax.experimental.pallas import tpu as pltpu
from jax.sharding import PartitionSpec as P

WIN = 256
HALF = WIN // 2
STEPS = 2
EPS = 1e-05
MASKED = -1000000000.0
EXCL = WIN // 4
STEP_K = 4
GROUP = 32
UNITS = 2
LANES = 128
ALIGN = 8
SMALL_LIMIT = 8 << 20


def sent(block, axis, target):
    count = lax.axis_size(axis)
    return lax.ppermute(block, axis, [(i, target(i, count)) for i in range(count)])


LINE = 4


def first_step(i, count):
    return (i + (2, 2, -1, 1)[i % LINE]) % count


def second_step(i, count):
    if i < LINE:
        return (1, 2, LINE, 0)[i]
    if i == count - 2:
        return count - 1
    return i + (-1, 1, 2, -2)[i % LINE]


def third_step(i, count):
    return i ^ 1


def across(distance):
    return lambda i, count: i ^ distance


def window_sums(src_m, bufs, span):
    size = 128
    src_v = None
    length = 1
    level = 0
    while length < HALF:
        dst_m, dst_v = bufs[level % 2]

        def step(p, carry, src_m=src_m, src_v=src_v, dst_m=dst_m, dst_v=dst_v, length=length):
            base = pl.multiple_of(p * size, size)
            m0 = src_m[pl.ds(base, size), :]
            m1 = src_m[pl.ds(base + length, size), :]
            gap = m0 - m1
            spread = gap * gap * (0.5 * length)
            if src_v is not None:
                spread = spread + (src_v[pl.ds(base, size), :] + src_v[pl.ds(base + length, size), :])
            dst_m[pl.ds(base, size), :] = (m0 + m1) * 0.5
            dst_v[pl.ds(base, size), :] = spread
            return carry

        lax.fori_loop(0, span // size, step, 0)
        src_m, src_v = dst_m, dst_v
        length *= 2
        level += 1
    return src_m, src_v, bufs[level % 2]


def contract(base, x8, mean_ref, scale_ref, zr, out, fill):
    rows = zr.shape[2]
    size = out.shape[0]
    first_row = STEPS * rows

    def windows(at, step):
        mean = mean_ref[pl.ds(at, GROUP), :]
        scale = scale_ref[pl.ds(at, GROUP), :]
        lag = lax.rem(step, 2) * STEP_K
        start = pl.multiple_of(step // 2 * ALIGN + at, ALIGN)
        z = []
        for k in range(STEP_K):
            x = x8[lag + k, pl.ds(start, GROUP), :]
            z.append(((x - mean) * scale).astype(jnp.bfloat16))
        return jnp.concatenate(z[:2], axis=1), jnp.concatenate(z[2:], axis=1)

    def stage(step):
        if fill:
            for at in range(0, rows, GROUP):
                for unit, z in enumerate(windows(first_row + at, step)):
                    zr[step, unit, at : at + GROUP, :] = z
        for unit in range(UNITS):
            pltpu.matmul_push_rhs(zr[step, unit], 0, unit, transpose=True)

    def run(*sums):
        sums = sums[: len(sums) // UNITS], sums[len(sums) // UNITS :]

        def stream(step, following):
            for g, at in enumerate(range(0, size, GROUP)):
                pair = windows(pl.multiple_of(base + at, GROUP), step)
                for unit in range(UNITS):
                    pltpu.matmul_acc_lhs(sums[unit][g], pair[unit], 0 if g == 0 else None)
                if g == 0 and following:
                    stage(step + 1)

        for g in range(size // GROUP):
            for unit in range(UNITS):
                pltpu.matmul_pop(sums[unit][g])
        steps = HALF // STEP_K
        stage(0)

        def advance(step, carry):
            stream(step, True)
            return carry

        lax.fori_loop(0, steps - 1, advance, 0)
        stream(steps - 1, False)
        for g, at in enumerate(range(0, size, GROUP)):
            both = pltpu.matmul_pop(sums[0][g]) + pltpu.matmul_pop(sums[1][g])
            out[at : at + GROUP, :] = both.astype(out.dtype)

    pl.run_scoped(run, *[pltpu.ACC(unit)((GROUP, rows), jnp.float32) for unit in range(UNITS) for _ in range(size // GROUP)])


def prepare(at_block, left, right, x8, end_m, end_v, work):
    x2, ma, mb, va, vb = work
    rows = left.shape[1]
    span = rows + HALF
    first = at_block * rows
    joined = jnp.concatenate([left, right], axis=1)
    both = jnp.concatenate([joined[:, :span], joined[:, HALF : HALF + span]], axis=0)
    for at in range(0, span, LANES):
        x2[at : at + LANES, :] = both[:, at : at + LANES].T
    src_m, src_v, _ = window_sums(x2, [(ma, va), (mb, vb)], span)
    for at in range(0, rows, LANES):
        m0 = src_m[at : at + LANES, :]
        v0 = src_v[at : at + LANES, :]
        m1 = pltpu.roll(m0, LANES // 2, 1)
        v1 = pltpu.roll(v0, LANES // 2, 1)
        gap = m0 - m1
        var = (v0 + v1 + gap * gap * (0.5 * HALF)) * (1.0 / WIN)
        end_m[first + at : first + at + LANES, :] = (m0 + m1) * 0.5
        end_v[first + at : first + at + LANES, :] = lax.rsqrt(var + EPS)
    held = span if at_block == STEPS else rows
    for s in range(ALIGN):
        for at in range(0, held, LANES):
            x8[s, first + at : first + at + LANES, :] = x2[at + s : at + s + LANES, :]


def neighbours(place, from_first, from_third, from_second=None, handed_on=None):
    second = from_first if from_second is None else from_second
    handed_on = from_first if handed_on is None else handed_on
    earlier = jnp.where(place == 0, second, jnp.where(place == 1, handed_on, from_first))
    odd = lax.rem(place, 2) == 1
    before = jnp.where(odd, from_third, jnp.where(place == 0, from_first, second))
    after = jnp.where(odd, jnp.where(place == 1, from_first, second), from_third)
    return earlier, before, after


def early_kernel(own, from_first, from_third, x8, end_m, end_v, *work):
    place = lax.rem(lax.axis_index("tm"), LINE)

    @pl.when(place < 2)
    def _():
        _, before, after = neighbours(place, from_first[...], from_third[...])
        prepare(1, before, own[...], x8, end_m, end_v, work)
        prepare(2, own[...], after, x8, end_m, end_v, work)


def far_kernel(own, from_first, from_third, from_second, handed_on, _x8, _m, _v, out, x8, end_m, end_v, zr, *work):
    place = lax.rem(lax.axis_index("tm"), LINE)
    earlier, before, after = neighbours(place, from_first[...], from_third[...], from_second[...], handed_on[...])
    prepare(0, earlier, before, x8, end_m, end_v, work)

    @pl.when(place >= 2)
    def _():
        prepare(1, before, own[...], x8, end_m, end_v, work)
        prepare(2, own[...], after, x8, end_m, end_v, work)

    base = (1 - lax.axis_index("chan") // 2) * out.shape[0]
    contract(base, x8, end_m, end_v, zr, out, True)


def near_kernel(x8, end_m, end_v, zr, out):
    base = lax.axis_index("chan") // 2 * out.shape[0]
    contract(base, x8, end_m, end_v, zr, out, False)


def peak_kernel(rows, lens, p0, p1, p2, p3, out):
    quarter = p0.shape[0]
    block = lax.axis_index("tm")
    part = lax.axis_index("chan") // 2
    last = rows * lax.axis_size("tm") - WIN
    seg = rows // 2
    start = (block - STEPS) * rows
    f32 = jnp.float32
    score = (p0[...] + p1[...]) + (p2[...].astype(f32) + p3[...].astype(f32))
    shape = (quarter, LANES)
    j = part * quarter + lax.broadcasted_iota(jnp.int32, shape, 0)
    stop = jnp.zeros(shape, jnp.int32)
    for s in range(2 * (STEPS + 1)):
        which = (block - STEPS) * 2 + s
        length = jnp.where(which >= 0, lens[jnp.maximum(which, 0)], 0)
        end = jnp.minimum(s * seg + length, last + 1 - start)
        stop = jnp.where(j >= s * seg, end, stop)
    reach = jnp.where(j < stop, j + EXCL, 2 * (STEPS + 1) * rows)
    lane = lax.broadcasted_iota(jnp.int32, shape, 1)
    for at in range(0, rows, LANES):
        i = lane + (STEPS * rows + at)
        best = jnp.max(jnp.where(i >= reach, score[:, at : at + LANES], MASKED), axis=0, keepdims=True)
        best = jnp.where(best > 0.5 * MASKED, best * (1.0 / WIN), MASKED)
        r = i[:1, :] - STEPS * rows
        own = jnp.where(r < seg, lens[block * 2], seg + lens[block * 2 + 1])
        out[:, at : at + LANES] = jnp.where(r < jnp.minimum(own, last + 1 - block * rows), best, MASKED)


def body(series, lengths):
    chans, rows = series.shape
    total = (STEPS + 1) * rows
    cols = total - EXCL
    side = cols // 2
    own = jnp.maximum(series, jnp.finfo(series.dtype).min)
    from_first = sent(series, "tm", first_step)
    from_second = sent(series, "tm", second_step)
    from_third = sent(series, "tm", third_step)
    handed_on = sent(from_first, "tm", third_step)
    vmem = pl.BlockSpec(memory_space=pltpu.VMEM)
    smem = pl.BlockSpec(memory_space=pltpu.SMEM)
    f32 = jnp.float32
    bf16 = jnp.bfloat16
    room = total + HALF + HALF
    tall = jax.ShapeDtypeStruct((room, LANES), f32)
    shifted = jax.ShapeDtypeStruct((ALIGN, room, LANES), f32)
    work = [pltpu.VMEM((rows + 2 * HALF, LANES), f32)] * 5
    early = pl.pallas_call(
        early_kernel,
        out_shape=[shifted, tall, tall],
        in_specs=[vmem] * 3,
        out_specs=[vmem] * 3,
        scratch_shapes=work,
        compiler_params=pltpu.CompilerParams(vmem_limit_bytes=SMALL_LIMIT),
    )(own, from_first, from_third)
    far, *shared = pl.pallas_call(
        far_kernel,
        out_shape=[
            jax.ShapeDtypeStruct((side, rows), bf16),
            shifted,
            tall,
            tall,
            jax.ShapeDtypeStruct((HALF // STEP_K, UNITS, rows, 2 * LANES), bf16),
        ],
        in_specs=[vmem] * 8,
        out_specs=[vmem] * 5,
        input_output_aliases={5: 1, 6: 2, 7: 3},
        scratch_shapes=work,
        compiler_params=pltpu.CompilerParams(vmem_limit_bytes=SMALL_LIMIT),
    )(own, from_first, from_third, from_second, handed_on, *early)
    far_got = sent(far, "chan", across(2))
    near = pl.pallas_call(
        near_kernel,
        out_shape=jax.ShapeDtypeStruct((side, rows), f32),
        in_specs=[vmem] * 4,
        out_specs=vmem,
        compiler_params=pltpu.CompilerParams(vmem_limit_bytes=SMALL_LIMIT),
    )(*shared)
    near_peer = sent(near, "chan", across(1))
    far_peer = sent(far_got, "chan", across(1))
    best = pl.pallas_call(
        functools.partial(peak_kernel, rows),
        out_shape=jax.ShapeDtypeStruct((1, rows), f32),
        in_specs=[smem] + [vmem] * 4,
        out_specs=vmem,
        compiler_params=pltpu.CompilerParams(vmem_limit_bytes=SMALL_LIMIT),
    )(lengths, near, near_peer, far_got, far_peer)
    best = jnp.maximum(best, sent(best, "chan", across(2)))
    return jnp.where(best > 0.5 * MASKED, best, 0.0).reshape(rows)


def solution(mesh):
    return jax.shard_map(
        body,
        mesh=mesh,
        in_specs=(P("chan", "tm"), P()),
        out_specs=P("tm"),
        check_vma=False,
    )
```

```python
import functools

import jax
import jax.numpy as jnp
from jax import lax
from jax.experimental import pallas as pl
from jax.experimental.pallas import tpu as pltpu
from jax.sharding import PartitionSpec as P

WIN = 256
HALF = WIN // 2
STEPS = 2
EPS = 1e-05
MASKED = -1000000000.0
EXCL = WIN // 4
STEP_K = 4
GROUP = 32
UNITS = 2
LANES = 128
ALIGN = 8
SMALL_LIMIT = 8 << 20


def sent(block, axis, target):
    count = lax.axis_size(axis)
    return lax.ppermute(block, axis, [(i, target(i, count)) for i in range(count)])


LINE = 4


def first_step(i, count):
    return (i + (2, 2, -1, 1)[i % LINE]) % count


def second_step(i, count):
    if i == 0:
        return 1
    if i == count - 2:
        return count - 1
    if i == count - 1:
        return 0
    return i + (-1, 1, 2, 2)[i % LINE]


def third_step(i, count):
    return i ^ 1


def across(distance):
    return lambda i, count: i ^ distance


def window_sums(src_m, bufs, span):
    size = 128
    src_v = None
    length = 1
    level = 0
    while length < HALF:
        dst_m, dst_v = bufs[level % 2]

        def step(p, carry, src_m=src_m, src_v=src_v, dst_m=dst_m, dst_v=dst_v, length=length):
            base = pl.multiple_of(p * size, size)
            m0 = src_m[pl.ds(base, size), :]
            m1 = src_m[pl.ds(base + length, size), :]
            gap = m0 - m1
            spread = gap * gap * (0.5 * length)
            if src_v is not None:
                spread = spread + (src_v[pl.ds(base, size), :] + src_v[pl.ds(base + length, size), :])
            dst_m[pl.ds(base, size), :] = (m0 + m1) * 0.5
            dst_v[pl.ds(base, size), :] = spread
            return carry

        lax.fori_loop(0, span // size, step, 0)
        src_m, src_v = dst_m, dst_v
        length *= 2
        level += 1
    return src_m, src_v, bufs[level % 2]


def windows(at, step, x8, mean_ref, scale_ref):
    mean = mean_ref[pl.ds(at, GROUP), :]
    scale = scale_ref[pl.ds(at, GROUP), :]
    lag = lax.rem(step, 2) * STEP_K
    start = pl.multiple_of(step // 2 * ALIGN + at, ALIGN)
    z = []
    for k in range(STEP_K):
        x = x8[lag + k, pl.ds(start, GROUP), :]
        z.append(((x - mean) * scale).astype(jnp.bfloat16))
    return jnp.concatenate(z[:2], axis=1), jnp.concatenate(z[2:], axis=1)


def fill_rows(step, x8, mean_ref, scale_ref, zr):
    rows = zr.shape[2]
    for at in range(0, rows, GROUP):
        for unit, z in enumerate(windows(STEPS * rows + at, step, x8, mean_ref, scale_ref)):
            zr[step, unit, at : at + GROUP, :] = z


def reaches(base, size, rows):
    return base + size > (STEPS - lax.axis_index("tm")) * rows


def contract(base, x8, mean_ref, scale_ref, zr, out, fill):
    rows = zr.shape[2]
    size = out.shape[0]

    def stage(step):
        if fill:
            fill_rows(step, x8, mean_ref, scale_ref, zr)
        for unit in range(UNITS):
            pltpu.matmul_push_rhs(zr[step, unit], 0, unit, transpose=True)

    def run(*sums):
        sums = sums[: len(sums) // UNITS], sums[len(sums) // UNITS :]

        def stream(step, following):
            for g, at in enumerate(range(0, size, GROUP)):
                pair = windows(pl.multiple_of(base + at, GROUP), step, x8, mean_ref, scale_ref)
                for unit in range(UNITS):
                    pltpu.matmul_acc_lhs(sums[unit][g], pair[unit], 0 if g == 0 else None)
                if g == 0 and following:
                    stage(step + 1)

        for g in range(size // GROUP):
            for unit in range(UNITS):
                pltpu.matmul_pop(sums[unit][g])
        steps = HALF // STEP_K
        stage(0)

        def advance(step, carry):
            stream(step, True)
            return carry

        lax.fori_loop(0, steps - 1, advance, 0)
        stream(steps - 1, False)
        for g, at in enumerate(range(0, size, GROUP)):
            both = pltpu.matmul_pop(sums[0][g]) + pltpu.matmul_pop(sums[1][g])
            out[at : at + GROUP, :] = both.astype(out.dtype)

    pl.run_scoped(run, *[pltpu.ACC(unit)((GROUP, rows), jnp.float32) for unit in range(UNITS) for _ in range(size // GROUP)])


def prepare(at_block, left, right, x8, end_m, end_v, work):
    x2, ma, mb, va, vb = work
    rows = left.shape[1]
    span = rows + HALF
    first = at_block * rows
    joined = jnp.concatenate([left, right], axis=1)
    both = jnp.concatenate([joined[:, :span], joined[:, HALF : HALF + span]], axis=0)
    for at in range(0, span, LANES):
        x2[at : at + LANES, :] = both[:, at : at + LANES].T
    src_m, src_v, _ = window_sums(x2, [(ma, va), (mb, vb)], span)
    for at in range(0, rows, LANES):
        m0 = src_m[at : at + LANES, :]
        v0 = src_v[at : at + LANES, :]
        m1 = pltpu.roll(m0, LANES // 2, 1)
        v1 = pltpu.roll(v0, LANES // 2, 1)
        gap = m0 - m1
        var = (v0 + v1 + gap * gap * (0.5 * HALF)) * (1.0 / WIN)
        end_m[first + at : first + at + LANES, :] = (m0 + m1) * 0.5
        end_v[first + at : first + at + LANES, :] = lax.rsqrt(var + EPS)
    held = span if at_block == STEPS else rows
    for s in range(ALIGN):
        for at in range(0, held, LANES):
            x8[s, first + at : first + at + LANES, :] = x2[at + s : at + s + LANES, :]


def neighbours(place, from_first, from_second, from_third):
    earlier = jnp.where(place < 2, from_second, from_first)
    odd = lax.rem(place, 2) == 1
    before = jnp.where(odd, from_third, jnp.where(place == 0, from_first, from_second))
    after = jnp.where(odd, jnp.where(place == 1, from_first, from_second), from_third)
    return earlier, before, after


def first_kernel(own, from_first, x8, end_m, end_v, *work):
    place = lax.rem(lax.axis_index("tm"), LINE)

    @pl.when(place == 0)
    def _():
        prepare(1, from_first[...], own[...], x8, end_m, end_v, work)

    @pl.when(place == 1)
    def _():
        prepare(2, own[...], from_first[...], x8, end_m, end_v, work)


def third_kernel(own, from_third, _x8, _m, _v, x8, end_m, end_v, zr, *work):
    place = lax.rem(lax.axis_index("tm"), LINE)

    @pl.when(place == 0)
    def _():
        prepare(2, own[...], from_third[...], x8, end_m, end_v, work)

    @pl.when(place == 1)
    def _():
        prepare(1, from_third[...], own[...], x8, end_m, end_v, work)

    @pl.when(place < 2)
    def _():
        def step(p, carry):
            fill_rows(p, x8, end_m, end_v, zr)
            return carry

        lax.fori_loop(0, zr.shape[0], step, 0)


def far_kernel(own, from_first, from_third, from_second, _x8, _m, _v, _zr, out, x8, end_m, end_v, zr, *work):
    place = lax.rem(lax.axis_index("tm"), LINE)
    size = out.shape[0]
    base = (1 - lax.axis_index("chan") // 2) * size
    live = reaches(base, size, own.shape[1])

    @pl.when(place < 2)
    def _():
        prepare(0, from_second[...], jnp.where(place == 0, from_first[...], from_third[...]), x8, end_m, end_v, work)

        @pl.when(live)
        def _():
            contract(base, x8, end_m, end_v, zr, out, False)

        @pl.when(jnp.logical_not(live))
        def _():
            out[...] = jnp.zeros_like(out)

    @pl.when(place >= 2)
    def _():
        earlier, before, after = neighbours(place, from_first[...], from_second[...], from_third[...])
        prepare(0, earlier, before, x8, end_m, end_v, work)
        prepare(1, before, own[...], x8, end_m, end_v, work)
        prepare(2, own[...], after, x8, end_m, end_v, work)
        contract(base, x8, end_m, end_v, zr, out, True)


def near_kernel(x8, end_m, end_v, zr, out):
    size = out.shape[0]
    base = lax.axis_index("chan") // 2 * size
    live = reaches(base, size, zr.shape[2])

    @pl.when(live)
    def _():
        contract(base, x8, end_m, end_v, zr, out, False)

    @pl.when(jnp.logical_not(live))
    def _():
        out[...] = jnp.zeros_like(out)


def peak_kernel(rows, lens, p0, p1, p2, p3, out):
    quarter = p0.shape[0]
    block = lax.axis_index("tm")
    part = lax.axis_index("chan") // 2
    last = rows * lax.axis_size("tm") - WIN
    seg = rows // 2
    start = (block - STEPS) * rows
    f32 = jnp.float32
    score = (p0[...] + p1[...]) + (p2[...].astype(f32) + p3[...].astype(f32))
    shape = (quarter, LANES)
    j = part * quarter + lax.broadcasted_iota(jnp.int32, shape, 0)
    stop = jnp.zeros(shape, jnp.int32)
    for s in range(2 * (STEPS + 1)):
        which = (block - STEPS) * 2 + s
        length = jnp.where(which >= 0, lens[jnp.maximum(which, 0)], 0)
        end = jnp.minimum(s * seg + length, last + 1 - start)
        stop = jnp.where(j >= s * seg, end, stop)
    reach = jnp.where(j < stop, j + EXCL, 2 * (STEPS + 1) * rows)
    lane = lax.broadcasted_iota(jnp.int32, shape, 1)
    for at in range(0, rows, LANES):
        i = lane + (STEPS * rows + at)
        best = jnp.max(jnp.where(i >= reach, score[:, at : at + LANES], MASKED), axis=0, keepdims=True)
        best = jnp.where(best > 0.5 * MASKED, best * (1.0 / WIN), MASKED)
        r = i[:1, :] - STEPS * rows
        own = jnp.where(r < seg, lens[block * 2], seg + lens[block * 2 + 1])
        out[:, at : at + LANES] = jnp.where(r < jnp.minimum(own, last + 1 - block * rows), best, MASKED)


def body(series, lengths):
    chans, rows = series.shape
    total = (STEPS + 1) * rows
    cols = total - EXCL
    side = cols // 2
    own = jnp.maximum(series, jnp.finfo(series.dtype).min)
    from_first = sent(series, "tm", first_step)
    from_second = sent(series, "tm", second_step)
    from_third = sent(series, "tm", third_step)
    vmem = pl.BlockSpec(memory_space=pltpu.VMEM)
    smem = pl.BlockSpec(memory_space=pltpu.SMEM)
    f32 = jnp.float32
    bf16 = jnp.bfloat16
    room = total + HALF + HALF
    tall = jax.ShapeDtypeStruct((room, LANES), f32)
    shifted = jax.ShapeDtypeStruct((ALIGN, room, LANES), f32)
    work = [pltpu.VMEM((rows + 2 * HALF, LANES), f32)] * 5
    row_windows = jax.ShapeDtypeStruct((HALF // STEP_K, UNITS, rows, 2 * LANES), bf16)
    params = pltpu.CompilerParams(vmem_limit_bytes=SMALL_LIMIT)
    after_first = pl.pallas_call(
        first_kernel,
        out_shape=[shifted, tall, tall],
        in_specs=[vmem] * 2,
        out_specs=[vmem] * 3,
        scratch_shapes=work,
        compiler_params=params,
    )(own, from_first)
    after_third = pl.pallas_call(
        third_kernel,
        out_shape=[shifted, tall, tall, row_windows],
        in_specs=[vmem] * 5,
        out_specs=[vmem] * 4,
        input_output_aliases={2: 0, 3: 1, 4: 2},
        scratch_shapes=work,
        compiler_params=params,
    )(own, from_third, *after_first)
    far, *shared = pl.pallas_call(
        far_kernel,
        out_shape=[jax.ShapeDtypeStruct((side, rows), bf16), shifted, tall, tall, row_windows],
        in_specs=[vmem] * 8,
        out_specs=[vmem] * 5,
        input_output_aliases={4: 1, 5: 2, 6: 3, 7: 4},
        scratch_shapes=work,
        compiler_params=params,
    )(own, from_first, from_third, from_second, *after_third)
    far_got = sent(far, "chan", across(2))
    near = pl.pallas_call(
        near_kernel,
        out_shape=jax.ShapeDtypeStruct((side, rows), f32),
        in_specs=[vmem] * 4,
        out_specs=vmem,
        compiler_params=pltpu.CompilerParams(vmem_limit_bytes=SMALL_LIMIT),
    )(*shared)
    near_peer = sent(near, "chan", across(1))
    far_peer = sent(far_got, "chan", across(1))
    best = pl.pallas_call(
        functools.partial(peak_kernel, rows),
        out_shape=jax.ShapeDtypeStruct((1, rows), f32),
        in_specs=[smem] + [vmem] * 4,
        out_specs=vmem,
        compiler_params=pltpu.CompilerParams(vmem_limit_bytes=SMALL_LIMIT),
    )(lengths, near, near_peer, far_got, far_peer)
    best = jnp.maximum(best, sent(best, "chan", across(2)))
    return jnp.where(best > 0.5 * MASKED, best, 0.0).reshape(rows)


def solution(mesh):
    return jax.shard_map(
        body,
        mesh=mesh,
        in_specs=(P("chan", "tm"), P()),
        out_specs=P("tm"),
        check_vma=False,
    )
```

```python
import functools

import jax
import jax.numpy as jnp
from jax import lax
from jax.experimental import pallas as pl
from jax.experimental.pallas import tpu as pltpu
from jax.sharding import PartitionSpec as P

WIN = 256
HALF = WIN // 2
STEPS = 2
EPS = 1e-05
MASKED = -1000000000.0
EXCL = WIN // 4
STEP_K = 4
GROUP = 32
UNITS = 2
LANES = 128
ALIGN = 8
SMALL_LIMIT = 8 << 20


def sent(block, axis, target):
    count = lax.axis_size(axis)
    return lax.ppermute(block, axis, [(i, target(i, count)) for i in range(count)])


LINE = 4


def first_step(i, count):
    return (i + (2, 2, -1, 1)[i % LINE]) % count


def second_step(i, count):
    if i == 0:
        return 1
    if i == count - 2:
        return count - 1
    if i == count - 1:
        return 0
    return i + (-1, 1, 2, 2)[i % LINE]


def third_step(i, count):
    return i ^ 1


def across(distance):
    return lambda i, count: i ^ distance


def window_sums(src_m, bufs, span):
    size = 128
    src_v = None
    length = 1
    level = 0
    while length < HALF:
        dst_m, dst_v = bufs[level % 2]

        def step(p, carry, src_m=src_m, src_v=src_v, dst_m=dst_m, dst_v=dst_v, length=length):
            base = pl.multiple_of(p * size, size)
            m0 = src_m[pl.ds(base, size), :]
            m1 = src_m[pl.ds(base + length, size), :]
            gap = m0 - m1
            spread = gap * gap * (0.5 * length)
            if src_v is not None:
                spread = spread + (src_v[pl.ds(base, size), :] + src_v[pl.ds(base + length, size), :])
            dst_m[pl.ds(base, size), :] = (m0 + m1) * 0.5
            dst_v[pl.ds(base, size), :] = spread
            return carry

        lax.fori_loop(0, span // size, step, 0)
        src_m, src_v = dst_m, dst_v
        length *= 2
        level += 1
    return src_m, src_v, bufs[level % 2]


def windows(at, two, half, x8, mean_ref, scale_ref):
    mean = mean_ref[pl.ds(at, GROUP), :]
    scale = scale_ref[pl.ds(at, GROUP), :]
    lag = half * STEP_K
    start = pl.multiple_of(two * ALIGN + at, ALIGN)
    z = []
    for k in range(STEP_K):
        x = x8[lag + k, pl.ds(start, GROUP), :]
        z.append(((x - mean) * scale).astype(jnp.bfloat16))
    return jnp.concatenate(z[:2], axis=1), jnp.concatenate(z[2:], axis=1)


def fill_rows(two, half, x8, mean_ref, scale_ref, zr):
    rows = zr.shape[2]
    step = 2 * two + half
    for at in range(0, rows, GROUP):
        for unit, z in enumerate(windows(STEPS * rows + at, two, half, x8, mean_ref, scale_ref)):
            zr[step, unit, at : at + GROUP, :] = z


def reaches(base, size, rows):
    return base + size > (STEPS - lax.axis_index("tm")) * rows


def contract(base, x8, mean_ref, scale_ref, zr, out, fill):
    rows = zr.shape[2]
    size = out.shape[0]

    def stage(two, half):
        step = 2 * two + half
        if fill:
            fill_rows(two, half, x8, mean_ref, scale_ref, zr)
        for unit in range(UNITS):
            pltpu.matmul_push_rhs(zr[step, unit], 0, unit, transpose=True)

    def run(*sums):
        sums = sums[: len(sums) // UNITS], sums[len(sums) // UNITS :]

        def stream(two, half, following):
            for g, at in enumerate(range(0, size, GROUP)):
                pair = windows(pl.multiple_of(base + at, GROUP), two, half, x8, mean_ref, scale_ref)
                for unit in range(UNITS):
                    pltpu.matmul_acc_lhs(sums[unit][g], pair[unit], 0 if g == 0 else None)
                if g == 0 and following is not None:
                    stage(*following)

        for g in range(size // GROUP):
            for unit in range(UNITS):
                pltpu.matmul_pop(sums[unit][g])
        twos = HALF // STEP_K // 2
        stage(0, 0)

        def advance(two, carry):
            stream(two, 0, (two, 1))
            stream(two, 1, (two + 1, 0))
            return carry

        lax.fori_loop(0, twos - 1, advance, 0)
        stream(twos - 1, 0, (twos - 1, 1))
        stream(twos - 1, 1, None)
        for g, at in enumerate(range(0, size, GROUP)):
            both = pltpu.matmul_pop(sums[0][g]) + pltpu.matmul_pop(sums[1][g])
            out[at : at + GROUP, :] = both.astype(out.dtype)

    pl.run_scoped(run, *[pltpu.ACC(unit)((GROUP, rows), jnp.float32) for unit in range(UNITS) for _ in range(size // GROUP)])


def prepare(at_block, left, right, x8, end_m, end_v, work):
    x2, ma, mb, va, vb = work
    rows = left.shape[1]
    span = rows + HALF
    first = at_block * rows
    joined = jnp.concatenate([left, right], axis=1)
    both = jnp.concatenate([joined[:, :span], joined[:, HALF : HALF + span]], axis=0)
    for at in range(0, span, LANES):
        x2[at : at + LANES, :] = both[:, at : at + LANES].T
    src_m, src_v, _ = window_sums(x2, [(ma, va), (mb, vb)], span)
    for at in range(0, rows, LANES):
        m0 = src_m[at : at + LANES, :]
        v0 = src_v[at : at + LANES, :]
        m1 = pltpu.roll(m0, LANES // 2, 1)
        v1 = pltpu.roll(v0, LANES // 2, 1)
        gap = m0 - m1
        var = (v0 + v1 + gap * gap * (0.5 * HALF)) * (1.0 / WIN)
        end_m[first + at : first + at + LANES, :] = (m0 + m1) * 0.5
        end_v[first + at : first + at + LANES, :] = lax.rsqrt(var + EPS)
    held = span if at_block == STEPS else rows
    for s in range(ALIGN):
        for at in range(0, held, LANES):
            x8[s, first + at : first + at + LANES, :] = x2[at + s : at + s + LANES, :]


def neighbours(place, from_first, from_second, from_third):
    earlier = jnp.where(place < 2, from_second, from_first)
    odd = lax.rem(place, 2) == 1
    before = jnp.where(odd, from_third, jnp.where(place == 0, from_first, from_second))
    after = jnp.where(odd, jnp.where(place == 1, from_first, from_second), from_third)
    return earlier, before, after


def first_kernel(own, from_first, x8, end_m, end_v, *work):
    place = lax.rem(lax.axis_index("tm"), LINE)

    @pl.when((place == 0) & (lax.axis_index("tm") > 0))
    def _():
        prepare(1, from_first[...], own[...], x8, end_m, end_v, work)

    @pl.when(place == 1)
    def _():
        prepare(2, own[...], from_first[...], x8, end_m, end_v, work)


def third_kernel(own, from_third, _x8, _m, _v, x8, end_m, end_v, zr, *work):
    place = lax.rem(lax.axis_index("tm"), LINE)

    @pl.when(place == 0)
    def _():
        prepare(2, own[...], from_third[...], x8, end_m, end_v, work)

    @pl.when(place == 1)
    def _():
        prepare(1, from_third[...], own[...], x8, end_m, end_v, work)

    @pl.when(place < 2)
    def _():
        def step(p, carry):
            fill_rows(p, 0, x8, end_m, end_v, zr)
            fill_rows(p, 1, x8, end_m, end_v, zr)
            return carry

        lax.fori_loop(0, zr.shape[0] // 2, step, 0)


def far_kernel(own, from_first, from_third, from_second, _x8, _m, _v, _zr, out, x8, end_m, end_v, zr, *work):
    place = lax.rem(lax.axis_index("tm"), LINE)
    size = out.shape[0]
    base = (1 - lax.axis_index("chan") // 2) * size
    live = reaches(base, size, own.shape[1])

    @pl.when(place < 2)
    def _():
        @pl.when(lax.axis_index("tm") > 1)
        def _():
            prepare(0, from_second[...], jnp.where(place == 0, from_first[...], from_third[...]), x8, end_m, end_v, work)

        @pl.when(live)
        def _():
            contract(base, x8, end_m, end_v, zr, out, False)

        @pl.when(jnp.logical_not(live))
        def _():
            out[...] = jnp.zeros_like(out)

    @pl.when(place >= 2)
    def _():
        earlier, before, after = neighbours(place, from_first[...], from_second[...], from_third[...])
        prepare(0, earlier, before, x8, end_m, end_v, work)
        prepare(1, before, own[...], x8, end_m, end_v, work)
        prepare(2, own[...], after, x8, end_m, end_v, work)
        contract(base, x8, end_m, end_v, zr, out, True)


def near_kernel(x8, end_m, end_v, zr, out):
    size = out.shape[0]
    base = lax.axis_index("chan") // 2 * size
    live = reaches(base, size, zr.shape[2])

    @pl.when(live)
    def _():
        contract(base, x8, end_m, end_v, zr, out, False)

    @pl.when(jnp.logical_not(live))
    def _():
        out[...] = jnp.zeros_like(out)


def peak_kernel(rows, lens, p0, p1, p2, p3, out):
    quarter = p0.shape[0]
    block = lax.axis_index("tm")
    part = lax.axis_index("chan") // 2
    last = rows * lax.axis_size("tm") - WIN
    seg = rows // 2
    start = (block - STEPS) * rows
    f32 = jnp.float32
    score = (p0[...] + p1[...]) + (p2[...].astype(f32) + p3[...].astype(f32))
    shape = (quarter, LANES)
    j = part * quarter + lax.broadcasted_iota(jnp.int32, shape, 0)
    stop = jnp.zeros(shape, jnp.int32)
    for s in range(2 * (STEPS + 1)):
        which = (block - STEPS) * 2 + s
        length = jnp.where(which >= 0, lens[jnp.maximum(which, 0)], 0)
        end = jnp.minimum(s * seg + length, last + 1 - start)
        stop = jnp.where(j >= s * seg, end, stop)
    reach = jnp.where(j < stop, j + EXCL, 2 * (STEPS + 1) * rows)
    lane = lax.broadcasted_iota(jnp.int32, shape, 1)
    for at in range(0, rows, LANES):
        i = lane + (STEPS * rows + at)
        best = jnp.max(jnp.where(i >= reach, score[:, at : at + LANES], MASKED), axis=0, keepdims=True)
        best = jnp.where(best > 0.5 * MASKED, best * (1.0 / WIN), MASKED)
        r = i[:1, :] - STEPS * rows
        own = jnp.where(r < seg, lens[block * 2], seg + lens[block * 2 + 1])
        out[:, at : at + LANES] = jnp.where(r < jnp.minimum(own, last + 1 - block * rows), best, MASKED)


def body(series, lengths):
    chans, rows = series.shape
    total = (STEPS + 1) * rows
    cols = total - EXCL
    side = cols // 2
    own = jnp.maximum(series, jnp.finfo(series.dtype).min)
    from_first = sent(series, "tm", first_step)
    from_second = sent(series, "tm", second_step)
    from_third = sent(series, "tm", third_step)
    vmem = pl.BlockSpec(memory_space=pltpu.VMEM)
    smem = pl.BlockSpec(memory_space=pltpu.SMEM)
    f32 = jnp.float32
    bf16 = jnp.bfloat16
    room = total + HALF + HALF
    tall = jax.ShapeDtypeStruct((room, LANES), f32)
    shifted = jax.ShapeDtypeStruct((ALIGN, room, LANES), f32)
    work = [pltpu.VMEM((rows + 2 * HALF, LANES), f32)] * 5
    row_windows = jax.ShapeDtypeStruct((HALF // STEP_K, UNITS, rows, 2 * LANES), bf16)
    params = pltpu.CompilerParams(vmem_limit_bytes=SMALL_LIMIT)
    after_first = pl.pallas_call(
        first_kernel,
        out_shape=[shifted, tall, tall],
        in_specs=[vmem] * 2,
        out_specs=[vmem] * 3,
        scratch_shapes=work,
        compiler_params=params,
    )(own, from_first)
    after_third = pl.pallas_call(
        third_kernel,
        out_shape=[shifted, tall, tall, row_windows],
        in_specs=[vmem] * 5,
        out_specs=[vmem] * 4,
        input_output_aliases={2: 0, 3: 1, 4: 2},
        scratch_shapes=work,
        compiler_params=params,
    )(own, from_third, *after_first)
    far, *shared = pl.pallas_call(
        far_kernel,
        out_shape=[jax.ShapeDtypeStruct((side, rows), bf16), shifted, tall, tall, row_windows],
        in_specs=[vmem] * 8,
        out_specs=[vmem] * 5,
        input_output_aliases={4: 1, 5: 2, 6: 3, 7: 4},
        scratch_shapes=work,
        compiler_params=params,
    )(own, from_first, from_third, from_second, *after_third)
    far_got = sent(far, "chan", across(2))
    near = pl.pallas_call(
        near_kernel,
        out_shape=jax.ShapeDtypeStruct((side, rows), f32),
        in_specs=[vmem] * 4,
        out_specs=vmem,
        compiler_params=pltpu.CompilerParams(vmem_limit_bytes=SMALL_LIMIT),
    )(*shared)
    near_peer = sent(near, "chan", across(1))
    far_peer = sent(far_got, "chan", across(1))
    best = pl.pallas_call(
        functools.partial(peak_kernel, rows),
        out_shape=jax.ShapeDtypeStruct((1, rows), f32),
        in_specs=[smem] + [vmem] * 4,
        out_specs=vmem,
        compiler_params=pltpu.CompilerParams(vmem_limit_bytes=SMALL_LIMIT),
    )(lengths, near, near_peer, far_got, far_peer)
    best = jnp.maximum(best, sent(best, "chan", across(2)))
    return jnp.where(best > 0.5 * MASKED, best, 0.0).reshape(rows)


def solution(mesh):
    return jax.shard_map(
        body,
        mesh=mesh,
        in_specs=(P("chan", "tm"), P()),
        out_specs=P("tm"),
        check_vma=False,
    )
```

```python
import functools

import jax
import jax.numpy as jnp
from jax import lax
from jax.experimental import pallas as pl
from jax.experimental.pallas import tpu as pltpu
from jax.sharding import PartitionSpec as P

WIN = 256
HALF = WIN // 2
STEPS = 2
EPS = 1e-05
MASKED = -1000000000.0
EXCL = WIN // 4
STEP_K = 4
GROUP = 32
UNITS = 2
BODY = 4
LANES = 128
ALIGN = 8
SMALL_LIMIT = 8 << 20


def sent(block, axis, target):
    count = lax.axis_size(axis)
    return lax.ppermute(block, axis, [(i, target(i, count)) for i in range(count)])


LINE = 4


def first_step(i, count):
    return (i + (2, 2, -1, 1)[i % LINE]) % count


def second_step(i, count):
    if i == 0:
        return 1
    if i == count - 2:
        return count - 1
    if i == count - 1:
        return 0
    return i + (-1, 1, 2, 2)[i % LINE]


def third_step(i, count):
    return i ^ 1


def across(distance):
    return lambda i, count: i ^ distance


def window_sums(src_m, bufs, span):
    size = 128
    src_v = None
    length = 1
    level = 0
    while length < HALF:
        dst_m, dst_v = bufs[level % 2]

        def step(p, carry, src_m=src_m, src_v=src_v, dst_m=dst_m, dst_v=dst_v, length=length):
            base = pl.multiple_of(p * size, size)
            m0 = src_m[pl.ds(base, size), :]
            m1 = src_m[pl.ds(base + length, size), :]
            gap = m0 - m1
            spread = gap * gap * (0.5 * length)
            if src_v is not None:
                spread = spread + (src_v[pl.ds(base, size), :] + src_v[pl.ds(base + length, size), :])
            dst_m[pl.ds(base, size), :] = (m0 + m1) * 0.5
            dst_v[pl.ds(base, size), :] = spread
            return carry

        lax.fori_loop(0, span // size, step, 0)
        src_m, src_v = dst_m, dst_v
        length *= 2
        level += 1
    return src_m, src_v, bufs[level % 2]


def windows(at, two, half, x8, mean_ref, scale_ref):
    mean = mean_ref[pl.ds(at, GROUP), :]
    scale = scale_ref[pl.ds(at, GROUP), :]
    lag = half * STEP_K
    start = pl.multiple_of(two * ALIGN + at, ALIGN)
    z = []
    for k in range(STEP_K):
        x = x8[lag + k, pl.ds(start, GROUP), :]
        z.append(((x - mean) * scale).astype(jnp.bfloat16))
    return jnp.concatenate(z[:2], axis=1), jnp.concatenate(z[2:], axis=1)


def fill_rows(two, half, x8, mean_ref, scale_ref, zr):
    rows = zr.shape[2]
    step = 2 * two + half
    for at in range(0, rows, GROUP):
        for unit, z in enumerate(windows(STEPS * rows + at, two, half, x8, mean_ref, scale_ref)):
            zr[step, unit, at : at + GROUP, :] = z


def reaches(base, size, rows):
    return base + size > (STEPS - lax.axis_index("tm")) * rows


def contract(base, x8, mean_ref, scale_ref, zr, out, fill):
    rows = zr.shape[2]
    size = out.shape[0]

    def stage(two, half):
        step = 2 * two + half
        if fill:
            fill_rows(two, half, x8, mean_ref, scale_ref, zr)
        for unit in range(UNITS):
            pltpu.matmul_push_rhs(zr[step, unit], 0, unit, transpose=True)

    def run(*sums):
        sums = sums[: len(sums) // UNITS], sums[len(sums) // UNITS :]

        def stream(two, half, following):
            for g, at in enumerate(range(0, size, GROUP)):
                pair = windows(pl.multiple_of(base + at, GROUP), two, half, x8, mean_ref, scale_ref)
                for unit in range(UNITS):
                    pltpu.matmul_acc_lhs(sums[unit][g], pair[unit], 0 if g == 0 else None)
                if g == 0 and following is not None:
                    stage(*following)

        for g in range(size // GROUP):
            for unit in range(UNITS):
                pltpu.matmul_pop(sums[unit][g])
        twos = HALF // STEP_K // 2
        stage(0, 0)

        def several(two, ends):
            for t in range(BODY):
                stream(two + t, 0, (two + t, 1))
                stream(two + t, 1, None if ends and t == BODY - 1 else (two + t + 1, 0))

        def advance(p, carry):
            several(p * BODY, False)
            return carry

        lax.fori_loop(0, twos // BODY - 1, advance, 0)
        several(twos - BODY, True)
        for g, at in enumerate(range(0, size, GROUP)):
            both = pltpu.matmul_pop(sums[0][g]) + pltpu.matmul_pop(sums[1][g])
            out[at : at + GROUP, :] = both.astype(out.dtype)

    pl.run_scoped(run, *[pltpu.ACC(unit)((GROUP, rows), jnp.float32) for unit in range(UNITS) for _ in range(size // GROUP)])


def prepare(at_block, left, right, x8, end_m, end_v, work):
    x2, ma, mb, va, vb = work
    rows = left.shape[1]
    span = rows + HALF
    first = at_block * rows
    joined = jnp.concatenate([left, right], axis=1)
    both = jnp.concatenate([joined[:, :span], joined[:, HALF : HALF + span]], axis=0)
    for at in range(0, span, LANES):
        x2[at : at + LANES, :] = both[:, at : at + LANES].T
    src_m, src_v, _ = window_sums(x2, [(ma, va), (mb, vb)], span)
    for at in range(0, rows, LANES):
        m0 = src_m[at : at + LANES, :]
        v0 = src_v[at : at + LANES, :]
        m1 = pltpu.roll(m0, LANES // 2, 1)
        v1 = pltpu.roll(v0, LANES // 2, 1)
        gap = m0 - m1
        var = (v0 + v1 + gap * gap * (0.5 * HALF)) * (1.0 / WIN)
        end_m[first + at : first + at + LANES, :] = (m0 + m1) * 0.5
        end_v[first + at : first + at + LANES, :] = lax.rsqrt(var + EPS)
    held = span if at_block == STEPS else rows
    for s in range(ALIGN):
        for at in range(0, held, LANES):
            x8[s, first + at : first + at + LANES, :] = x2[at + s : at + s + LANES, :]


def neighbours(place, from_first, from_second, from_third):
    earlier = jnp.where(place < 2, from_second, from_first)
    odd = lax.rem(place, 2) == 1
    before = jnp.where(odd, from_third, jnp.where(place == 0, from_first, from_second))
    after = jnp.where(odd, jnp.where(place == 1, from_first, from_second), from_third)
    return earlier, before, after


def first_kernel(own, from_first, x8, end_m, end_v, *work):
    place = lax.rem(lax.axis_index("tm"), LINE)

    @pl.when((place == 0) & (lax.axis_index("tm") > 0))
    def _():
        prepare(1, from_first[...], own[...], x8, end_m, end_v, work)

    @pl.when(place == 1)
    def _():
        prepare(2, own[...], from_first[...], x8, end_m, end_v, work)


def third_kernel(own, from_third, _x8, _m, _v, x8, end_m, end_v, zr, *work):
    place = lax.rem(lax.axis_index("tm"), LINE)

    @pl.when(place == 0)
    def _():
        prepare(2, own[...], from_third[...], x8, end_m, end_v, work)

    @pl.when(place == 1)
    def _():
        prepare(1, from_third[...], own[...], x8, end_m, end_v, work)

    @pl.when(place < 2)
    def _():
        def step(p, carry):
            fill_rows(p, 0, x8, end_m, end_v, zr)
            fill_rows(p, 1, x8, end_m, end_v, zr)
            return carry

        lax.fori_loop(0, zr.shape[0] // 2, step, 0)


def far_kernel(own, from_first, from_third, from_second, _x8, _m, _v, _zr, out, x8, end_m, end_v, zr, *work):
    place = lax.rem(lax.axis_index("tm"), LINE)
    size = out.shape[0]
    base = (1 - lax.axis_index("chan") // 2) * size
    live = reaches(base, size, own.shape[1])

    @pl.when(place < 2)
    def _():
        @pl.when(lax.axis_index("tm") > 1)
        def _():
            prepare(0, from_second[...], jnp.where(place == 0, from_first[...], from_third[...]), x8, end_m, end_v, work)

        @pl.when(live)
        def _():
            contract(base, x8, end_m, end_v, zr, out, False)

        @pl.when(jnp.logical_not(live))
        def _():
            out[...] = jnp.zeros_like(out)

    @pl.when(place >= 2)
    def _():
        earlier, before, after = neighbours(place, from_first[...], from_second[...], from_third[...])
        prepare(0, earlier, before, x8, end_m, end_v, work)
        prepare(1, before, own[...], x8, end_m, end_v, work)
        prepare(2, own[...], after, x8, end_m, end_v, work)
        contract(base, x8, end_m, end_v, zr, out, True)


def near_kernel(x8, end_m, end_v, zr, out):
    size = out.shape[0]
    base = lax.axis_index("chan") // 2 * size
    live = reaches(base, size, zr.shape[2])

    @pl.when(live)
    def _():
        contract(base, x8, end_m, end_v, zr, out, False)

    @pl.when(jnp.logical_not(live))
    def _():
        out[...] = jnp.zeros_like(out)


def peak_kernel(rows, lens, p0, p1, p2, p3, out):
    quarter = p0.shape[0]
    block = lax.axis_index("tm")
    part = lax.axis_index("chan") // 2
    last = rows * lax.axis_size("tm") - WIN
    seg = rows // 2
    start = (block - STEPS) * rows
    f32 = jnp.float32
    score = (p0[...] + p1[...]) + (p2[...].astype(f32) + p3[...].astype(f32))
    shape = (quarter, LANES)
    j = part * quarter + lax.broadcasted_iota(jnp.int32, shape, 0)
    stop = jnp.zeros(shape, jnp.int32)
    for s in range(2 * (STEPS + 1)):
        which = (block - STEPS) * 2 + s
        length = jnp.where(which >= 0, lens[jnp.maximum(which, 0)], 0)
        end = jnp.minimum(s * seg + length, last + 1 - start)
        stop = jnp.where(j >= s * seg, end, stop)
    reach = jnp.where(j < stop, j + EXCL, 2 * (STEPS + 1) * rows)
    lane = lax.broadcasted_iota(jnp.int32, shape, 1)
    for at in range(0, rows, LANES):
        i = lane + (STEPS * rows + at)
        best = jnp.max(jnp.where(i >= reach, score[:, at : at + LANES], MASKED), axis=0, keepdims=True)
        best = jnp.where(best > 0.5 * MASKED, best * (1.0 / WIN), MASKED)
        r = i[:1, :] - STEPS * rows
        own = jnp.where(r < seg, lens[block * 2], seg + lens[block * 2 + 1])
        out[:, at : at + LANES] = jnp.where(r < jnp.minimum(own, last + 1 - block * rows), best, MASKED)


def body(series, lengths):
    chans, rows = series.shape
    total = (STEPS + 1) * rows
    cols = total - EXCL
    side = cols // 2
    own = jnp.maximum(series, jnp.finfo(series.dtype).min)
    from_first = sent(series, "tm", first_step)
    from_second = sent(series, "tm", second_step)
    from_third = sent(series, "tm", third_step)
    vmem = pl.BlockSpec(memory_space=pltpu.VMEM)
    smem = pl.BlockSpec(memory_space=pltpu.SMEM)
    f32 = jnp.float32
    bf16 = jnp.bfloat16
    room = total + HALF + HALF
    tall = jax.ShapeDtypeStruct((room, LANES), f32)
    shifted = jax.ShapeDtypeStruct((ALIGN, room, LANES), f32)
    work = [pltpu.VMEM((rows + 2 * HALF, LANES), f32)] * 5
    row_windows = jax.ShapeDtypeStruct((HALF // STEP_K, UNITS, rows, 2 * LANES), bf16)
    params = pltpu.CompilerParams(vmem_limit_bytes=SMALL_LIMIT)
    after_first = pl.pallas_call(
        first_kernel,
        out_shape=[shifted, tall, tall],
        in_specs=[vmem] * 2,
        out_specs=[vmem] * 3,
        scratch_shapes=work,
        compiler_params=params,
    )(own, from_first)
    after_third = pl.pallas_call(
        third_kernel,
        out_shape=[shifted, tall, tall, row_windows],
        in_specs=[vmem] * 5,
        out_specs=[vmem] * 4,
        input_output_aliases={2: 0, 3: 1, 4: 2},
        scratch_shapes=work,
        compiler_params=params,
    )(own, from_third, *after_first)
    far, *shared = pl.pallas_call(
        far_kernel,
        out_shape=[jax.ShapeDtypeStruct((side, rows), bf16), shifted, tall, tall, row_windows],
        in_specs=[vmem] * 8,
        out_specs=[vmem] * 5,
        input_output_aliases={4: 1, 5: 2, 6: 3, 7: 4},
        scratch_shapes=work,
        compiler_params=params,
    )(own, from_first, from_third, from_second, *after_third)
    far_got = sent(far, "chan", across(2))
    near = pl.pallas_call(
        near_kernel,
        out_shape=jax.ShapeDtypeStruct((side, rows), f32),
        in_specs=[vmem] * 4,
        out_specs=vmem,
        compiler_params=pltpu.CompilerParams(vmem_limit_bytes=SMALL_LIMIT),
    )(*shared)
    near_peer = sent(near, "chan", across(1))
    far_peer = sent(far_got, "chan", across(1))
    best = pl.pallas_call(
        functools.partial(peak_kernel, rows),
        out_shape=jax.ShapeDtypeStruct((1, rows), f32),
        in_specs=[smem] + [vmem] * 4,
        out_specs=vmem,
        compiler_params=pltpu.CompilerParams(vmem_limit_bytes=SMALL_LIMIT),
    )(lengths, near, near_peer, far_got, far_peer)
    best = jnp.maximum(best, sent(best, "chan", across(2)))
    return jnp.where(best > 0.5 * MASKED, best, 0.0).reshape(rows)


def solution(mesh):
    return jax.shard_map(
        body,
        mesh=mesh,
        in_specs=(P("chan", "tm"), P()),
        out_specs=P("tm"),
        check_vma=False,
    )
```

```python
import jax
import jax.numpy as jnp
from jax import lax
from jax.experimental import pallas as pl
from jax.experimental.pallas import tpu as pltpu
from jax.sharding import PartitionSpec as P

WIN = 256
HALF = WIN // 2
STEPS = 2
EPS = 1e-05
MASKED = -1000000000.0
EXCL = WIN // 4
STEP_K = 4
GROUP = 32
UNITS = 2
BODY = 4
LANES = 128
ALIGN = 8
SMALL_LIMIT = 8 << 20


def sent(block, axis, target):
    count = lax.axis_size(axis)
    return lax.ppermute(block, axis, [(i, target(i, count)) for i in range(count)])


LINE = 4


def first_step(i, count):
    return (i + (2, 2, -1, 1)[i % LINE]) % count


def second_step(i, count):
    if i == 0:
        return 1
    if i == count - 2:
        return count - 1
    if i == count - 1:
        return 0
    return i + (-1, 1, 2, 2)[i % LINE]


def third_step(i, count):
    return i ^ 1


def across(distance):
    return lambda i, count: i ^ distance


def window_sums(src_m, bufs, span):
    size = 128
    src_v = None
    length = 1
    level = 0
    while length < HALF:
        dst_m, dst_v = bufs[level % 2]

        def step(p, carry, src_m=src_m, src_v=src_v, dst_m=dst_m, dst_v=dst_v, length=length):
            base = pl.multiple_of(p * size, size)
            m0 = src_m[pl.ds(base, size), :]
            m1 = src_m[pl.ds(base + length, size), :]
            gap = m0 - m1
            spread = gap * gap * (0.5 * length)
            if src_v is not None:
                spread = spread + (src_v[pl.ds(base, size), :] + src_v[pl.ds(base + length, size), :])
            dst_m[pl.ds(base, size), :] = (m0 + m1) * 0.5
            dst_v[pl.ds(base, size), :] = spread
            return carry

        lax.fori_loop(0, span // size, step, 0)
        src_m, src_v = dst_m, dst_v
        length *= 2
        level += 1
    return src_m, src_v, bufs[level % 2]


def windows(at, two, half, x8, mean_ref, scale_ref):
    mean = mean_ref[pl.ds(at, GROUP), :]
    scale = scale_ref[pl.ds(at, GROUP), :]
    lag = half * STEP_K
    start = pl.multiple_of(two * ALIGN + at, ALIGN)
    z = []
    for k in range(STEP_K):
        x = x8[lag + k, pl.ds(start, GROUP), :]
        z.append(((x - mean) * scale).astype(jnp.bfloat16))
    return jnp.concatenate(z[:2], axis=1), jnp.concatenate(z[2:], axis=1)


def fill_rows(two, half, x8, mean_ref, scale_ref, zr):
    rows = zr.shape[2]
    step = 2 * two + half
    for at in range(0, rows, GROUP):
        for unit, z in enumerate(windows(STEPS * rows + at, two, half, x8, mean_ref, scale_ref)):
            zr[step, unit, at : at + GROUP, :] = z


def reaches(base, size, rows):
    return base + size > (STEPS - lax.axis_index("tm")) * rows


def contract(base, x8, mean_ref, scale_ref, zr, out, fill):
    rows = zr.shape[2]
    size = out.shape[0]

    def stage(two, half):
        step = 2 * two + half
        if fill:
            fill_rows(two, half, x8, mean_ref, scale_ref, zr)
        for unit in range(UNITS):
            pltpu.matmul_push_rhs(zr[step, unit], 0, unit, transpose=True)

    def run(*sums):
        sums = sums[: len(sums) // UNITS], sums[len(sums) // UNITS :]

        def stream(two, half, following):
            for g, at in enumerate(range(0, size, GROUP)):
                pair = windows(pl.multiple_of(base + at, GROUP), two, half, x8, mean_ref, scale_ref)
                for unit in range(UNITS):
                    pltpu.matmul_acc_lhs(sums[unit][g], pair[unit], 0 if g == 0 else None)
                if g == 0 and following is not None:
                    stage(*following)

        for g in range(size // GROUP):
            for unit in range(UNITS):
                pltpu.matmul_pop(sums[unit][g])
        twos = HALF // STEP_K // 2
        stage(0, 0)

        def several(two, ends):
            for t in range(BODY):
                stream(two + t, 0, (two + t, 1))
                stream(two + t, 1, None if ends and t == BODY - 1 else (two + t + 1, 0))

        def advance(p, carry):
            several(p * BODY, False)
            return carry

        lax.fori_loop(0, twos // BODY - 1, advance, 0)
        several(twos - BODY, True)
        for g, at in enumerate(range(0, size, GROUP)):
            both = pltpu.matmul_pop(sums[0][g]) + pltpu.matmul_pop(sums[1][g])
            out[at : at + GROUP, :] = both.astype(out.dtype)

    pl.run_scoped(run, *[pltpu.ACC(unit)((GROUP, rows), jnp.float32) for unit in range(UNITS) for _ in range(size // GROUP)])


def prepare(at_block, left, right, x8, end_m, end_v, work):
    x2, ma, mb, va, vb = work
    rows = left.shape[1]
    span = rows + HALF
    first = at_block * rows
    joined = jnp.concatenate([left, right], axis=1)
    both = jnp.concatenate([joined[:, :span], joined[:, HALF : HALF + span]], axis=0)
    for at in range(0, span, LANES):
        x2[at : at + LANES, :] = both[:, at : at + LANES].T
    src_m, src_v, _ = window_sums(x2, [(ma, va), (mb, vb)], span)
    for at in range(0, rows, LANES):
        m0 = src_m[at : at + LANES, :]
        v0 = src_v[at : at + LANES, :]
        m1 = pltpu.roll(m0, LANES // 2, 1)
        v1 = pltpu.roll(v0, LANES // 2, 1)
        gap = m0 - m1
        var = (v0 + v1 + gap * gap * (0.5 * HALF)) * (1.0 / WIN)
        end_m[first + at : first + at + LANES, :] = (m0 + m1) * 0.5
        end_v[first + at : first + at + LANES, :] = lax.rsqrt(var + EPS)
    held = span if at_block == STEPS else rows
    for s in range(ALIGN):
        for at in range(0, held, LANES):
            x8[s, first + at : first + at + LANES, :] = x2[at + s : at + s + LANES, :]


def neighbours(place, from_first, from_second, from_third):
    earlier = jnp.where(place < 2, from_second, from_first)
    odd = lax.rem(place, 2) == 1
    before = jnp.where(odd, from_third, jnp.where(place == 0, from_first, from_second))
    after = jnp.where(odd, jnp.where(place == 1, from_first, from_second), from_third)
    return earlier, before, after


def first_kernel(own, from_first, lens, x8, end_m, end_v, reach, row_ok, *work):
    limits(own.shape[1], lens, reach, row_ok)
    place = lax.rem(lax.axis_index("tm"), LINE)

    @pl.when((place == 0) & (lax.axis_index("tm") > 0))
    def _():
        prepare(1, from_first[...], own[...], x8, end_m, end_v, work)

    @pl.when(place == 1)
    def _():
        prepare(2, own[...], from_first[...], x8, end_m, end_v, work)


def third_kernel(own, from_third, _x8, _m, _v, x8, end_m, end_v, zr, *work):
    place = lax.rem(lax.axis_index("tm"), LINE)

    @pl.when(place == 0)
    def _():
        prepare(2, own[...], from_third[...], x8, end_m, end_v, work)

    @pl.when(place == 1)
    def _():
        prepare(1, from_third[...], own[...], x8, end_m, end_v, work)

    @pl.when(place < 2)
    def _():
        def step(p, carry):
            for t in range(BODY):
                fill_rows(p * BODY + t, 0, x8, end_m, end_v, zr)
                fill_rows(p * BODY + t, 1, x8, end_m, end_v, zr)
            return carry

        lax.fori_loop(0, zr.shape[0] // (2 * BODY), step, 0)


def far_kernel(own, from_first, from_third, from_second, _x8, _m, _v, _zr, out, x8, end_m, end_v, zr, *work):
    place = lax.rem(lax.axis_index("tm"), LINE)
    size = out.shape[0]
    base = (1 - lax.axis_index("chan") // 2) * size
    live = reaches(base, size, own.shape[1])

    @pl.when(place < 2)
    def _():
        @pl.when(lax.axis_index("tm") > 1)
        def _():
            prepare(0, from_second[...], jnp.where(place == 0, from_first[...], from_third[...]), x8, end_m, end_v, work)

        @pl.when(live)
        def _():
            contract(base, x8, end_m, end_v, zr, out, False)

        @pl.when(jnp.logical_not(live))
        def _():
            out[...] = jnp.zeros_like(out)

    @pl.when(place >= 2)
    def _():
        earlier, before, after = neighbours(place, from_first[...], from_second[...], from_third[...])
        prepare(0, earlier, before, x8, end_m, end_v, work)
        prepare(1, before, own[...], x8, end_m, end_v, work)
        prepare(2, own[...], after, x8, end_m, end_v, work)
        contract(base, x8, end_m, end_v, zr, out, True)


def near_kernel(x8, end_m, end_v, zr, out):
    size = out.shape[0]
    base = lax.axis_index("chan") // 2 * size
    live = reaches(base, size, zr.shape[2])

    @pl.when(live)
    def _():
        contract(base, x8, end_m, end_v, zr, out, False)

    @pl.when(jnp.logical_not(live))
    def _():
        out[...] = jnp.zeros_like(out)


def limits(rows, lens, reach, row_ok):
    quarter = reach.shape[0]
    block = lax.axis_index("tm")
    part = lax.axis_index("chan") // 2
    last = rows * lax.axis_size("tm") - WIN
    seg = rows // 2
    start = (block - STEPS) * rows
    j = part * quarter + lax.broadcasted_iota(jnp.int32, reach.shape, 0)
    stop = jnp.zeros(reach.shape, jnp.int32)
    for s in range(2 * (STEPS + 1)):
        which = (block - STEPS) * 2 + s
        length = jnp.where(which >= 0, lens[jnp.maximum(which, 0)], 0)
        end = jnp.minimum(s * seg + length, last + 1 - start)
        stop = jnp.where(j >= s * seg, end, stop)
    reach[...] = jnp.where(j < stop, j + EXCL, 2 * (STEPS + 1) * rows)
    r = lax.broadcasted_iota(jnp.int32, row_ok.shape, 1)
    own = jnp.where(r < seg, lens[block * 2], seg + lens[block * 2 + 1])
    row_ok[...] = jnp.where(r < jnp.minimum(own, last + 1 - block * rows), 1, 0)


def peak_kernel(reach, row_ok, p0, p1, p2, p3, out):
    rows = out.shape[1]
    f32 = jnp.float32
    first_row = reach[...]
    lane = lax.broadcasted_iota(jnp.int32, first_row.shape, 1)
    for at in range(0, rows, LANES):
        part = slice(at, at + LANES)
        score = (p0[:, part] + p1[:, part]) + (p2[:, part].astype(f32) + p3[:, part].astype(f32))
        i = lane + (STEPS * rows + at)
        best = jnp.max(jnp.where(i >= first_row, score, MASKED), axis=0, keepdims=True)
        best = jnp.where(best > 0.5 * MASKED, best * (1.0 / WIN), MASKED)
        out[:, part] = jnp.where(row_ok[:, part] > 0, best, MASKED)


def body(series, lengths):
    chans, rows = series.shape
    total = (STEPS + 1) * rows
    cols = total - EXCL
    side = cols // 2
    own = jnp.maximum(series, jnp.finfo(series.dtype).min)
    from_first = sent(series, "tm", first_step)
    from_second = sent(series, "tm", second_step)
    from_third = sent(series, "tm", third_step)
    vmem = pl.BlockSpec(memory_space=pltpu.VMEM)
    smem = pl.BlockSpec(memory_space=pltpu.SMEM)
    f32 = jnp.float32
    bf16 = jnp.bfloat16
    room = total + HALF + HALF
    tall = jax.ShapeDtypeStruct((room, LANES), f32)
    shifted = jax.ShapeDtypeStruct((ALIGN, room, LANES), f32)
    work = [pltpu.VMEM((rows + 2 * HALF, LANES), f32)] * 5
    row_windows = jax.ShapeDtypeStruct((HALF // STEP_K, UNITS, rows, 2 * LANES), bf16)
    params = pltpu.CompilerParams(vmem_limit_bytes=SMALL_LIMIT)
    *after_first, reach, row_ok = pl.pallas_call(
        first_kernel,
        out_shape=[
            shifted,
            tall,
            tall,
            jax.ShapeDtypeStruct((side, LANES), jnp.int32),
            jax.ShapeDtypeStruct((1, rows), jnp.int32),
        ],
        in_specs=[vmem, vmem, smem],
        out_specs=[vmem] * 5,
        scratch_shapes=work,
        compiler_params=params,
    )(own, from_first, lengths)
    after_third = pl.pallas_call(
        third_kernel,
        out_shape=[shifted, tall, tall, row_windows],
        in_specs=[vmem] * 5,
        out_specs=[vmem] * 4,
        input_output_aliases={2: 0, 3: 1, 4: 2},
        scratch_shapes=work,
        compiler_params=params,
    )(own, from_third, *after_first)
    far, *shared = pl.pallas_call(
        far_kernel,
        out_shape=[jax.ShapeDtypeStruct((side, rows), bf16), shifted, tall, tall, row_windows],
        in_specs=[vmem] * 8,
        out_specs=[vmem] * 5,
        input_output_aliases={4: 1, 5: 2, 6: 3, 7: 4},
        scratch_shapes=work,
        compiler_params=params,
    )(own, from_first, from_third, from_second, *after_third)
    far_got = sent(far, "chan", across(2))
    near = pl.pallas_call(
        near_kernel,
        out_shape=jax.ShapeDtypeStruct((side, rows), f32),
        in_specs=[vmem] * 4,
        out_specs=vmem,
        compiler_params=pltpu.CompilerParams(vmem_limit_bytes=SMALL_LIMIT),
    )(*shared)
    near_peer = sent(near, "chan", across(1))
    far_peer = sent(far_got, "chan", across(1))
    best = pl.pallas_call(
        peak_kernel,
        out_shape=jax.ShapeDtypeStruct((1, rows), f32),
        in_specs=[vmem] * 6,
        out_specs=vmem,
        compiler_params=pltpu.CompilerParams(vmem_limit_bytes=SMALL_LIMIT),
    )(reach, row_ok, near, near_peer, far_got, far_peer)
    best = jnp.maximum(best, sent(best, "chan", across(2)))
    return jnp.where(best > 0.5 * MASKED, best, 0.0).reshape(rows)


def solution(mesh):
    return jax.shard_map(
        body,
        mesh=mesh,
        in_specs=(P("chan", "tm"), P()),
        out_specs=P("tm"),
        check_vma=False,
    )
```

```python
import functools

import jax
import jax.numpy as jnp
from jax import lax
from jax.experimental import pallas as pl
from jax.experimental.pallas import tpu as pltpu
from jax.sharding import PartitionSpec as P

WIN = 256
HALF = WIN // 2
STEPS = 2
EPS = 1e-05
MASKED = -1000000000.0
EXCL = WIN // 4
STEP_K = 4
GROUP = 16
UNITS = 2
BODY = 4
LANES = 128
ALIGN = 8
SMALL_LIMIT = 8 << 20


def sent(block, axis, target):
    count = lax.axis_size(axis)
    return lax.ppermute(block, axis, [(i, target(i, count)) for i in range(count)])


LINE = 4


def first_step(i, count):
    return (i + (2, 2, -1, 1)[i % LINE]) % count


def second_step(i, count):
    if i == 0:
        return 1
    if i == count - 2:
        return count - 1
    if i == count - 1:
        return 0
    return i + (-1, 1, 2, 2)[i % LINE]


def third_step(i, count):
    return i ^ 1


def across(distance):
    return lambda i, count: i ^ distance


def window_sums(src_m, bufs, span):
    size = 128
    src_v = None
    length = 1
    level = 0
    while length < HALF:
        dst_m, dst_v = bufs[level % 2]

        def step(p, carry, src_m=src_m, src_v=src_v, dst_m=dst_m, dst_v=dst_v, length=length):
            base = pl.multiple_of(p * size, size)
            m0 = src_m[pl.ds(base, size), :]
            m1 = src_m[pl.ds(base + length, size), :]
            gap = m0 - m1
            spread = gap * gap * (0.5 * length)
            if src_v is not None:
                spread = spread + (src_v[pl.ds(base, size), :] + src_v[pl.ds(base + length, size), :])
            dst_m[pl.ds(base, size), :] = (m0 + m1) * 0.5
            dst_v[pl.ds(base, size), :] = spread
            return carry

        lax.fori_loop(0, span // size, step, 0)
        src_m, src_v = dst_m, dst_v
        length *= 2
        level += 1
    return src_m, src_v, bufs[level % 2]


def windows(at, two, half, x8, mean_ref, scale_ref):
    mean = mean_ref[pl.ds(at, GROUP), :]
    scale = scale_ref[pl.ds(at, GROUP), :]
    lag = half * STEP_K
    start = pl.multiple_of(two * ALIGN + at, ALIGN)
    z = []
    for k in range(STEP_K):
        x = x8[lag + k, pl.ds(start, GROUP), :]
        z.append(((x - mean) * scale).astype(jnp.bfloat16))
    return jnp.concatenate(z[:2], axis=1), jnp.concatenate(z[2:], axis=1)


def fill_rows(two, half, x8, mean_ref, scale_ref, zr):
    rows = zr.shape[2]
    step = 2 * two + half
    for at in range(0, rows, GROUP):
        for unit, z in enumerate(windows(STEPS * rows + at, two, half, x8, mean_ref, scale_ref)):
            zr[step, unit, at : at + GROUP, :] = z


def reaches(base, size, rows):
    return base + size > (STEPS - lax.axis_index("tm")) * rows


def contract(base, x8, mean_ref, scale_ref, zr, out, fill):
    rows = zr.shape[2]
    size = out.shape[0]

    def stage(two, half):
        step = 2 * two + half
        if fill:
            fill_rows(two, half, x8, mean_ref, scale_ref, zr)
        for unit in range(UNITS):
            pltpu.matmul_push_rhs(zr[step, unit], 0, unit, transpose=True)

    def run(*sums):
        sums = sums[: len(sums) // UNITS], sums[len(sums) // UNITS :]

        def stream(two, half, following):
            for g, at in enumerate(range(0, size, GROUP)):
                pair = windows(pl.multiple_of(base + at, GROUP), two, half, x8, mean_ref, scale_ref)
                for unit in range(UNITS):
                    pltpu.matmul_acc_lhs(sums[unit][g], pair[unit], 0 if g == 0 else None)
                if g == 0 and following is not None:
                    stage(*following)

        for g in range(size // GROUP):
            for unit in range(UNITS):
                pltpu.matmul_pop(sums[unit][g])
        twos = HALF // STEP_K // 2
        stage(0, 0)

        def several(two, ends):
            for t in range(BODY):
                stream(two + t, 0, (two + t, 1))
                stream(two + t, 1, None if ends and t == BODY - 1 else (two + t + 1, 0))

        def advance(p, carry):
            several(p * BODY, False)
            return carry

        lax.fori_loop(0, twos // BODY - 1, advance, 0)
        several(twos - BODY, True)
        for g, at in enumerate(range(0, size, GROUP)):
            both = pltpu.matmul_pop(sums[0][g]) + pltpu.matmul_pop(sums[1][g])
            out[at : at + GROUP, :] = both.astype(out.dtype)

    pl.run_scoped(run, *[pltpu.ACC(unit)((GROUP, rows), jnp.float32) for unit in range(UNITS) for _ in range(size // GROUP)])


def prepare(at_block, left, right, x8, end_m, end_v, work):
    x2, ma, mb, va, vb = work
    rows = left.shape[1]
    span = rows + HALF
    first = at_block * rows
    joined = jnp.concatenate([left, right], axis=1)
    both = jnp.concatenate([joined[:, :span], joined[:, HALF : HALF + span]], axis=0)
    for at in range(0, span, LANES):
        x2[at : at + LANES, :] = both[:, at : at + LANES].T
    src_m, src_v, _ = window_sums(x2, [(ma, va), (mb, vb)], span)
    for at in range(0, rows, LANES):
        m0 = src_m[at : at + LANES, :]
        v0 = src_v[at : at + LANES, :]
        m1 = pltpu.roll(m0, LANES // 2, 1)
        v1 = pltpu.roll(v0, LANES // 2, 1)
        gap = m0 - m1
        var = (v0 + v1 + gap * gap * (0.5 * HALF)) * (1.0 / WIN)
        end_m[first + at : first + at + LANES, :] = (m0 + m1) * 0.5
        end_v[first + at : first + at + LANES, :] = lax.rsqrt(var + EPS)
    held = span if at_block == STEPS else rows
    for s in range(ALIGN):
        for at in range(0, held, LANES):
            x8[s, first + at : first + at + LANES, :] = x2[at + s : at + s + LANES, :]


def neighbours(place, from_first, from_second, from_third):
    earlier = jnp.where(place < 2, from_second, from_first)
    odd = lax.rem(place, 2) == 1
    before = jnp.where(odd, from_third, jnp.where(place == 0, from_first, from_second))
    after = jnp.where(odd, jnp.where(place == 1, from_first, from_second), from_third)
    return earlier, before, after


def first_kernel(own, from_first, x8, end_m, end_v, *work):
    place = lax.rem(lax.axis_index("tm"), LINE)

    @pl.when((place == 0) & (lax.axis_index("tm") > 0))
    def _():
        prepare(1, from_first[...], own[...], x8, end_m, end_v, work)

    @pl.when(place == 1)
    def _():
        prepare(2, own[...], from_first[...], x8, end_m, end_v, work)


def third_kernel(own, from_third, _x8, _m, _v, x8, end_m, end_v, zr, *work):
    place = lax.rem(lax.axis_index("tm"), LINE)

    @pl.when(place == 0)
    def _():
        prepare(2, own[...], from_third[...], x8, end_m, end_v, work)

    @pl.when(place == 1)
    def _():
        prepare(1, from_third[...], own[...], x8, end_m, end_v, work)

    @pl.when(place < 2)
    def _():
        def step(p, carry):
            fill_rows(p, 0, x8, end_m, end_v, zr)
            fill_rows(p, 1, x8, end_m, end_v, zr)
            return carry

        lax.fori_loop(0, zr.shape[0] // 2, step, 0)


def far_kernel(own, from_first, from_third, from_second, _x8, _m, _v, _zr, out, x8, end_m, end_v, zr, *work):
    place = lax.rem(lax.axis_index("tm"), LINE)
    size = out.shape[0]
    base = (1 - lax.axis_index("chan") // 2) * size
    live = reaches(base, size, own.shape[1])

    @pl.when(place < 2)
    def _():
        @pl.when(lax.axis_index("tm") > 1)
        def _():
            prepare(0, from_second[...], jnp.where(place == 0, from_first[...], from_third[...]), x8, end_m, end_v, work)

        @pl.when(live)
        def _():
            contract(base, x8, end_m, end_v, zr, out, False)

        @pl.when(jnp.logical_not(live))
        def _():
            out[...] = jnp.zeros_like(out)

    @pl.when(place >= 2)
    def _():
        earlier, before, after = neighbours(place, from_first[...], from_second[...], from_third[...])
        prepare(0, earlier, before, x8, end_m, end_v, work)
        prepare(1, before, own[...], x8, end_m, end_v, work)
        prepare(2, own[...], after, x8, end_m, end_v, work)
        contract(base, x8, end_m, end_v, zr, out, True)


def near_kernel(x8, end_m, end_v, zr, out):
    size = out.shape[0]
    base = lax.axis_index("chan") // 2 * size
    live = reaches(base, size, zr.shape[2])

    @pl.when(live)
    def _():
        contract(base, x8, end_m, end_v, zr, out, False)

    @pl.when(jnp.logical_not(live))
    def _():
        out[...] = jnp.zeros_like(out)


def peak_kernel(rows, lens, p0, p1, p2, p3, out):
    quarter = p0.shape[0]
    block = lax.axis_index("tm")
    part = lax.axis_index("chan") // 2
    last = rows * lax.axis_size("tm") - WIN
    seg = rows // 2
    start = (block - STEPS) * rows
    f32 = jnp.float32
    score = (p0[...] + p1[...]) + (p2[...].astype(f32) + p3[...].astype(f32))
    shape = (quarter, LANES)
    j = part * quarter + lax.broadcasted_iota(jnp.int32, shape, 0)
    stop = jnp.zeros(shape, jnp.int32)
    for s in range(2 * (STEPS + 1)):
        which = (block - STEPS) * 2 + s
        length = jnp.where(which >= 0, lens[jnp.maximum(which, 0)], 0)
        end = jnp.minimum(s * seg + length, last + 1 - start)
        stop = jnp.where(j >= s * seg, end, stop)
    reach = jnp.where(j < stop, j + EXCL, 2 * (STEPS + 1) * rows)
    lane = lax.broadcasted_iota(jnp.int32, shape, 1)
    for at in range(0, rows, LANES):
        i = lane + (STEPS * rows + at)
        best = jnp.max(jnp.where(i >= reach, score[:, at : at + LANES], MASKED), axis=0, keepdims=True)
        best = jnp.where(best > 0.5 * MASKED, best * (1.0 / WIN), MASKED)
        r = i[:1, :] - STEPS * rows
        own = jnp.where(r < seg, lens[block * 2], seg + lens[block * 2 + 1])
        out[:, at : at + LANES] = jnp.where(r < jnp.minimum(own, last + 1 - block * rows), best, MASKED)


def body(series, lengths):
    chans, rows = series.shape
    total = (STEPS + 1) * rows
    cols = total - EXCL
    side = cols // 2
    own = jnp.maximum(series, jnp.finfo(series.dtype).min)
    from_first = sent(series, "tm", first_step)
    from_second = sent(series, "tm", second_step)
    from_third = sent(series, "tm", third_step)
    vmem = pl.BlockSpec(memory_space=pltpu.VMEM)
    smem = pl.BlockSpec(memory_space=pltpu.SMEM)
    f32 = jnp.float32
    bf16 = jnp.bfloat16
    room = total + HALF + HALF
    tall = jax.ShapeDtypeStruct((room, LANES), f32)
    shifted = jax.ShapeDtypeStruct((ALIGN, room, LANES), f32)
    work = [pltpu.VMEM((rows + 2 * HALF, LANES), f32)] * 5
    row_windows = jax.ShapeDtypeStruct((HALF // STEP_K, UNITS, rows, 2 * LANES), bf16)
    params = pltpu.CompilerParams(vmem_limit_bytes=SMALL_LIMIT)
    after_first = pl.pallas_call(
        first_kernel,
        out_shape=[shifted, tall, tall],
        in_specs=[vmem] * 2,
        out_specs=[vmem] * 3,
        scratch_shapes=work,
        compiler_params=params,
    )(own, from_first)
    after_third = pl.pallas_call(
        third_kernel,
        out_shape=[shifted, tall, tall, row_windows],
        in_specs=[vmem] * 5,
        out_specs=[vmem] * 4,
        input_output_aliases={2: 0, 3: 1, 4: 2},
        scratch_shapes=work,
        compiler_params=params,
    )(own, from_third, *after_first)
    far, *shared = pl.pallas_call(
        far_kernel,
        out_shape=[jax.ShapeDtypeStruct((side, rows), bf16), shifted, tall, tall, row_windows],
        in_specs=[vmem] * 8,
        out_specs=[vmem] * 5,
        input_output_aliases={4: 1, 5: 2, 6: 3, 7: 4},
        scratch_shapes=work,
        compiler_params=params,
    )(own, from_first, from_third, from_second, *after_third)
    far_got = sent(far, "chan", across(2))
    near = pl.pallas_call(
        near_kernel,
        out_shape=jax.ShapeDtypeStruct((side, rows), f32),
        in_specs=[vmem] * 4,
        out_specs=vmem,
        compiler_params=pltpu.CompilerParams(vmem_limit_bytes=SMALL_LIMIT),
    )(*shared)
    near_peer = sent(near, "chan", across(1))
    far_peer = sent(far_got, "chan", across(1))
    best = pl.pallas_call(
        functools.partial(peak_kernel, rows),
        out_shape=jax.ShapeDtypeStruct((1, rows), f32),
        in_specs=[smem] + [vmem] * 4,
        out_specs=vmem,
        compiler_params=pltpu.CompilerParams(vmem_limit_bytes=SMALL_LIMIT),
    )(lengths, near, near_peer, far_got, far_peer)
    best = jnp.maximum(best, sent(best, "chan", across(2)))
    return jnp.where(best > 0.5 * MASKED, best, 0.0).reshape(rows)


def solution(mesh):
    return jax.shard_map(
        body,
        mesh=mesh,
        in_specs=(P("chan", "tm"), P()),
        out_specs=P("tm"),
        check_vma=False,
    )
```
